32 devices in a mesh: tm: 8 (over z, x), space: 4 (over y, core).
Axes of the slice: x: 2, y: 2, z: 4, core: 2. Of those that a mesh axis runs over, the one named last changes fastest.
Arguments:
- snapshots: float32 [4224, 4096], P('tm', 'space')
- starts: int32 [32], replicated, may hold values from 0 to 3968, as said below
- freq_lines: int32 [128], replicated, may hold values from 0 to 128, as said below
Outputs:
- power_density: float32 [128, 4096], P(None, ('space', 'tm'))
- gram_matrices: float32 [2, 128, 32, 32], P(None, 'tm')
The draws below stay inside these ranges and needn't reach their ends.
Inputs may be any that keep to these rules, and one draw needn't show every extreme that they name: starts never fall, and block b starts at most 64 snapshots away from b * 128; the first block starts at 0 and the last at 3968. `freq_lines`: distinct line numbers in any order; 0 and 128 are among them.
All inputs are finite; a program needn't handle non-finite values.
Results may differ from the reference program's by a relative error of at most 0.0001.
Values sent between devices are 32-bit elements; how exact they have to be, the bound alone decides.
No kernel may reach another device: no remote copies, remote signals or barrier semaphores. Data moves between devices by JAX's collectives and lax.ppermute only.
A program may use at most 64 MiB of HBM per device.

```python
import math
import jax
import jax.numpy as jnp
from jax import lax

NFFT = 256
HOP = 128
NF = 128
NB = 32
TIMES = 4224
PTS_DEV = 128
TILE = 1024
POINTS = 4096


def draw_snapshots(key, part):
    keys = jax.random.split(key, 5)
    points = jnp.arange(POINTS, dtype=jnp.int32)
    moments = jnp.arange(TIMES, dtype=jnp.int32)
    in_tile = (points % TILE).astype(jnp.float32) / TILE
    in_slab = points.astype(jnp.float32) / POINTS
    trend = 0.5 * jnp.sqrt((1.0 + 2.0 * in_tile) * (1.0 + 2.0 * in_slab))
    noise = jax.random.normal(keys[0], (TIMES, POINTS), jnp.float32)
    rough = jnp.exp(jax.random.uniform(keys[1], (POINTS,), jnp.float32, math.log(0.2), math.log(2.0)))
    tone_line = jax.random.randint(keys[2], (POINTS,), 0, NFFT // 2 + 1)
    amplitude = jax.random.uniform(keys[3], (POINTS,), jnp.float32, 0.5, 1.5)
    phase_zero = jax.random.uniform(keys[4], (POINTS,), jnp.float32, -math.pi, math.pi)
    cycle = moments[:, None] * tone_line[None, :] % NFFT
    tone = amplitude[None, :] * jnp.cos(2.0 * math.pi / NFFT * cycle.astype(jnp.float32) + phase_zero[None, :])
    values = trend[None, :] * (rough[None, :] * noise + tone)
    return values.astype(jnp.float32)


def draw_starts(key, part):
    index = jnp.arange(NB, dtype=jnp.int32)
    jitter = jax.random.randint(key, (NB,), -(HOP // 2), HOP // 2 + 1)
    placed = jnp.clip(index * HOP + jitter, 0, TIMES - NFFT)
    placed = jnp.where(index == 0, 0, jnp.where(index == NB - 1, TIMES - NFFT, placed))
    return placed.astype(jnp.int32)


def draw_freq_lines(key, part):
    dropped = jax.random.randint(jax.random.fold_in(key, 3), (), 1, NF)
    index = jnp.arange(NF, dtype=jnp.int32)
    chosen = index + (index >= dropped).astype(jnp.int32)
    return jax.random.permutation(jax.random.fold_in(key, 7), chosen).astype(jnp.int32)


def setup_inputs(seed: int = 0) -> dict:
    key_of = jax.random.split(jax.random.key(seed), 4)
    return {
        "snapshots": draw_snapshots(jax.random.fold_in(key_of[3], 71), 0),
        "starts": draw_starts(jax.random.fold_in(key_of[3], 71), 0),
        "freq_lines": draw_freq_lines(jax.random.fold_in(key_of[3], 71), 0),
    }


def spectral_table(freq_lines):
    moments = jnp.arange(NFFT, dtype=jnp.int32)
    cycle = freq_lines[:, None] * moments[None, :] % NFFT
    angles = 2.0 * math.pi / NFFT * cycle.astype(jnp.float32)
    window = 0.5 - 0.5 * jnp.cos(2.0 * math.pi / NFFT * moments.astype(jnp.float32))
    window = window / jnp.sqrt(jnp.sum(window * window))
    return jnp.concatenate([window[None, :] * jnp.cos(angles), -window[None, :] * jnp.sin(angles)], axis=0)

def block_spectra(series, starts, table):
    offsets = starts[:, None] + jnp.arange(NFFT, dtype=jnp.int32)[None, :]
    blocks = series[offsets]
    return jnp.einsum('kt,btp->kbp', table, blocks, precision=lax.Precision.HIGHEST)

def local_terms(spectra, factor):
    highest = lax.Precision.HIGHEST
    real_part = spectra[:NF]
    imag_part = spectra[NF:]
    power = lax.optimization_barrier(jnp.sum(real_part * real_part + imag_part * imag_part, axis=1)) / NB
    gram_real = jnp.einsum('fbp,fcp->fbc', real_part, real_part, precision=highest) + jnp.einsum('fbp,fcp->fbc', imag_part, imag_part, precision=highest)
    gram_imag = jnp.einsum('fbp,fcp->fbc', real_part, imag_part, precision=highest) - jnp.einsum('fbp,fcp->fbc', imag_part, real_part, precision=highest)
    return (power, jnp.stack([gram_real, gram_imag]) * factor)

def reference(snapshots, starts, freq_lines):
    table = spectral_table(freq_lines)
    factor = 1.0 / (NB * POINTS)

    def advance(carry, column_index):
        series = lax.dynamic_slice_in_dim(snapshots, column_index * PTS_DEV, PTS_DEV, 1)
        power, gram_part = local_terms(block_spectra(series, starts, table), factor)
        return (carry + gram_part, power)
    initial = jnp.zeros((2, NF, NB, NB), jnp.float32)
    columns = jnp.arange(POINTS // PTS_DEV, dtype=jnp.int32)
    gram_matrices, powers = lax.scan(advance, initial, columns)
    power_density = jnp.transpose(powers, (1, 0, 2)).reshape(NF, POINTS)
    return (power_density, gram_matrices)
```

```python
import functools
import math

import jax
import jax.numpy as jnp
from jax import lax
from jax.experimental import pallas as pl
from jax.experimental.pallas import tpu as pltpu
from jax.sharding import PartitionSpec as P

NFFT = 256
NF = 128
NB = 32
LANES = 128
PACK = LANES // NB
F32 = jnp.float32
BF16 = jnp.bfloat16
VMEM = pltpu.VMEM
SMEM = pltpu.SMEM


def spectral_table(freq_lines):
    moments = jnp.arange(NFFT, dtype=jnp.int32)
    cycle = freq_lines[:, None] * moments[None, :] % NFFT
    angles = 2.0 * math.pi / NFFT * cycle.astype(jnp.float32)
    window = 0.5 - 0.5 * jnp.cos(2.0 * math.pi / NFFT * moments.astype(jnp.float32))
    window = window / jnp.sqrt(jnp.sum(window * window))
    return jnp.concatenate(
        [window[None, :] * jnp.cos(angles), -window[None, :] * jnp.sin(angles)], axis=0
    )


def split(x):
    high = x.astype(BF16)
    return high, (x - high.astype(F32)).astype(BF16)


def dft_kernel(starts_ref, table_ref, series_ref, spec_ref, power_ref, halves):
    high, low = split(table_ref[...])
    halves[:NFFT] = high
    halves[NFFT:] = low
    power_ref[...] = jnp.zeros_like(power_ref)

    def step(pair, carry):
        b = 2 * pair
        block = jnp.concatenate(
            [series_ref[pl.ds(starts_ref[b + i], NFFT), :] for i in range(2)], axis=1
        )
        x_high, x_low = split(block)
        both = jnp.dot(halves[...], x_high, preferred_element_type=F32)
        out = jnp.dot(halves[:NFFT], x_low, preferred_element_type=F32)
        out = out + both[:NFFT] + both[NFFT:]
        for i in range(2):
            part = out[:, i * LANES : (i + 1) * LANES]
            spec_ref[pl.ds(b + i, 2 * NF, stride=NB), :] = part
            square = part * part
            power_ref[...] += square[:NF] + square[NF:]
        return carry

    lax.fori_loop(0, NB // 2, step, 0, unroll=2)
    power_ref[...] = power_ref[...] * (1.0 / NB)


def block_spectra(starts, table, series):
    return pl.pallas_call(
        dft_kernel,
        name="dft",
        in_specs=[
            pl.BlockSpec(memory_space=SMEM),
            pl.BlockSpec(memory_space=VMEM),
            pl.BlockSpec(memory_space=VMEM),
        ],
        out_specs=[pl.BlockSpec(memory_space=VMEM)] * 2,
        out_shape=[
            jax.ShapeDtypeStruct((2 * NF * NB, LANES), F32),
            jax.ShapeDtypeStruct((NF, LANES), F32),
        ],
        scratch_shapes=[VMEM((2 * NFFT, NFFT), BF16)],
        compiler_params=pltpu.CompilerParams(vmem_limit_bytes=24 << 20),
        cost_estimate=pl.CostEstimate(
            flops=6 * 2 * NF * NFFT * NB * LANES, bytes_accessed=6 << 20, transcendentals=0
        ),
    )(starts, table, series)


def gram_kernel(count, first_ref, spec_ref, out_ref):
    rows = PACK * NB
    base = first_ref[0] * rows
    row = lax.broadcasted_iota(jnp.int32, (NB, LANES), 0)
    lane = lax.broadcasted_iota(jnp.int32, (NB, LANES), 1)
    upper = row <= lane % NB
    contract = (((1,), (1,)), ((), ()))
    for j in range(count):
        start = pl.multiple_of(base + j * rows, rows)
        spectra = jnp.concatenate(
            [spec_ref[pl.ds(start, rows), :], spec_ref[pl.ds(start + NF * NB, rows), :]], axis=1
        )
        high, low = split(spectra)
        turned = [
            jnp.concatenate([a, jnp.concatenate([a[:, LANES:], -a[:, :LANES]], axis=1)], axis=0)
            for a in (high, low)
        ]
        both = lax.dot_general(
            jnp.concatenate([high, low], axis=0), turned[0], contract, preferred_element_type=F32
        )
        full = lax.dot_general(high, turned[1], contract, preferred_element_type=F32)
        full = full + both[:rows] + both[rows:]
        packed = jnp.zeros((NB, LANES), F32)
        for i in range(PACK):
            mine = full[i * NB : (i + 1) * NB]
            chosen = jnp.where(upper, mine[:, :LANES], mine[:, LANES:])
            packed = jnp.where(lane // NB == i, chosen, packed)
        out_ref[j] = packed


def packed_grams(first, count, spec):
    return pl.pallas_call(
        functools.partial(gram_kernel, count),
        name="gram",
        in_specs=[pl.BlockSpec(memory_space=SMEM), pl.BlockSpec(memory_space=VMEM)],
        out_specs=pl.BlockSpec(memory_space=VMEM),
        out_shape=jax.ShapeDtypeStruct((count, NB, LANES), F32),
        compiler_params=pltpu.CompilerParams(vmem_limit_bytes=24 << 20),
        cost_estimate=pl.CostEstimate(
            flops=count * 6 * LANES * 4 * LANES * LANES * 2,
            bytes_accessed=count << 18,
            transcendentals=0,
        ),
    )(first.reshape(1), spec)


def unpack_kernel(count, factor, packed_ref, out_ref):
    row = lax.broadcasted_iota(jnp.int32, (NB, NB), 0)
    column = lax.broadcasted_iota(jnp.int32, (NB, NB), 1)
    for j in range(count):
        packed = packed_ref[j] * factor
        turned = packed.T
        for i in range(PACK):
            here = packed[:, i * NB : (i + 1) * NB]
            there = turned[i * NB : (i + 1) * NB, :]
            out_ref[0, j * PACK + i] = jnp.where(row <= column, here, there)
            out_ref[1, j * PACK + i] = jnp.where(
                row > column, here, jnp.where(row < column, -there, 0.0)
            )


def unpack(packed, factor):
    count = packed.shape[0]
    return pl.pallas_call(
        functools.partial(unpack_kernel, count, factor),
        name="unpack",
        in_specs=[pl.BlockSpec(memory_space=VMEM)],
        out_specs=pl.BlockSpec(memory_space=VMEM),
        out_shape=jax.ShapeDtypeStruct((2, count * PACK, NB, NB), F32),
    )(packed)


def summed_small(spec):
    tm = lax.axis_index("tm")
    core = lax.axis_index("space") % 2
    z, x = tm // 2, tm % 2
    groups = NF // PACK // 4

    def swap(value, axis, bits):
        size = lax.axis_size(axis)
        return lax.ppermute(value, axis, [(i, i ^ bits) for i in range(size)])

    terms = []
    for j in (2, 3, 1):
        part = packed_grams((z ^ j) * groups, groups, spec)
        terms.append(swap(part, "tm", 2 * j))
    total = packed_grams(z * groups, groups, spec)
    for term in terms:
        total = total + term
    total = total.reshape(2, 2, groups // 4, NB, LANES)
    kept = lax.dynamic_index_in_dim(total, core, 1, keepdims=False)
    sent = lax.dynamic_index_in_dim(total, 1 - core, 1, keepdims=False)
    kept = kept + swap(sent, "space", 1)
    mine = lax.dynamic_index_in_dim(kept, x, 0, keepdims=False)
    other = lax.dynamic_index_in_dim(kept, 1 - x, 0, keepdims=False)
    from_y = swap(mine, "space", 2)
    from_x = swap(other, "tm", 1)
    from_xy = lax.ppermute(
        other,
        ("tm", "space"),
        [(i * 4 + s, (i ^ 1) * 4 + (s ^ 2)) for i in range(8) for s in range(4)],
    )
    mine = mine + from_y + from_x + from_xy
    theirs = swap(mine, "space", 1)
    first = jnp.where(core == 0, mine, theirs)
    second = jnp.where(core == 0, theirs, mine)
    return jnp.concatenate([first, second], axis=0)


def summed_any(spec):
    packed = packed_grams(jnp.int32(0), NF // PACK, spec)
    own = lax.psum_scatter(packed, "tm", scatter_dimension=0, tiled=True)
    return lax.psum(own, "space")


def body(snapshots, starts, freq_lines):
    groups = lax.axis_size("tm")
    spaces = lax.axis_size("space")
    columns = snapshots.shape[1] // groups
    table = spectral_table(freq_lines)
    arranged = snapshots.reshape(snapshots.shape[0], groups, columns)
    series = lax.all_to_all(arranged, "tm", split_axis=1, concat_axis=0, tiled=True)[:, 0, :]
    spec, power_density = block_spectra(starts, table, series)
    if (groups, spaces) == (8, 4):
        own = summed_small(spec)
    else:
        own = summed_any(spec)
    factor = 1.0 / (NB * columns * groups * spaces)
    return power_density, unpack(own, factor)


def solution(mesh):
    placed = (P("tm", "space"), P(), P())
    return jax.shard_map(
        body,
        mesh=mesh,
        in_specs=placed,
        out_specs=(P(None, ("space", "tm")), P(None, "tm", None, None)),
        check_vma=False,
    )
```

```python
import functools
import math

import jax
import jax.numpy as jnp
from jax import lax
from jax.experimental import pallas as pl
from jax.experimental.pallas import tpu as pltpu
from jax.sharding import PartitionSpec as P

NFFT = 256
NF = 128
NB = 32
LANES = 128
PACK = LANES // NB
PITCH = NB + 8
CORE_STEP = 2
F32 = jnp.float32
BF16 = jnp.bfloat16
VMEM = pltpu.VMEM
SMEM = pltpu.SMEM


def spectral_table(freq_lines):
    moments = jnp.arange(NFFT, dtype=jnp.int32)
    cycle = freq_lines[:, None] * moments[None, :] % NFFT
    angles = 2.0 * math.pi / NFFT * cycle.astype(jnp.float32)
    window = 0.5 - 0.5 * jnp.cos(2.0 * math.pi / NFFT * moments.astype(jnp.float32))
    window = window / jnp.sqrt(jnp.sum(window * window))
    return jnp.concatenate(
        [window[None, :] * jnp.cos(angles), -window[None, :] * jnp.sin(angles)], axis=0
    )


def split(x):
    high = x.astype(BF16)
    return high, (x - high.astype(F32)).astype(BF16)


def dft_kernel(count, rows, where_ref, starts_ref, table_ref, *refs):
    pieces, (spec_ref, power_ref, halves, series) = refs[:count], refs[count:]
    for k in range(count):
        start = pl.multiple_of(where_ref[k] * rows, 8)
        series[pl.ds(start, rows), :] = pieces[k][...]
    high, low = split(table_ref[...])
    halves[:NFFT] = high
    halves[NFFT:] = low
    power_ref[...] = jnp.zeros_like(power_ref)

    def step(pair, carry):
        b = 2 * pair
        block = jnp.concatenate(
            [series[pl.ds(starts_ref[b + i], NFFT), :] for i in range(2)], axis=1
        )
        x_high, x_low = split(block)
        both = jnp.dot(halves[...], x_high, preferred_element_type=F32)
        out = jnp.dot(halves[:NFFT], x_low, preferred_element_type=F32)
        out = out + both[:NFFT] + both[NFFT:]
        for i in range(2):
            part = out[:, i * LANES : (i + 1) * LANES]
            spec_ref[pl.ds(b + i, 2 * NF, stride=PITCH), :] = part
            square = part * part
            power_ref[...] += square[:NF] + square[NF:]
        return carry

    lax.fori_loop(0, NB // 2, step, 0, unroll=4)
    power_ref[...] = power_ref[...] * (1.0 / NB)


def block_spectra(starts, table, pieces, where):
    count, rows = len(pieces), pieces[0].shape[0]
    return pl.pallas_call(
        functools.partial(dft_kernel, count, rows),
        name="dft",
        in_specs=[pl.BlockSpec(memory_space=SMEM)] * 2
        + [pl.BlockSpec(memory_space=VMEM)] * (1 + count),
        out_specs=[pl.BlockSpec(memory_space=VMEM)] * 2,
        out_shape=[
            jax.ShapeDtypeStruct((2 * NF * PITCH, LANES), F32),
            jax.ShapeDtypeStruct((NF, LANES), F32),
        ],
        scratch_shapes=[VMEM((2 * NFFT, NFFT), BF16), VMEM((count * rows, LANES), F32)],
        compiler_params=pltpu.CompilerParams(vmem_limit_bytes=24 << 20),
        cost_estimate=pl.CostEstimate(
            flops=6 * 2 * NF * NFFT * NB * LANES, bytes_accessed=6 << 20, transcendentals=0
        ),
    )(where, starts, table, *pieces)


def gram_kernel(order, first_ref, core_ref, spec_ref, *out_refs):
    rows = PACK * NB
    row = lax.broadcasted_iota(jnp.int32, (NB, LANES), 0)
    lane = lax.broadcasted_iota(jnp.int32, (NB, LANES), 1)
    upper = row <= lane % NB
    contract = (((1,), (1,)), ((), ()))
    for j, place in order:
        for out_ref, group in zip(out_refs, (j + core_ref[0] * CORE_STEP, j + (1 - core_ref[0]) * CORE_STEP)):
            line = (first_ref[0] + group) * PACK
            starts = [pl.multiple_of((line + i) * PITCH, 8) for i in range(PACK)]
            spectra = jnp.concatenate(
                [
                    jnp.concatenate([spec_ref[pl.ds(s + part * NF * PITCH, NB), :] for s in starts], axis=0)
                    for part in range(2)
                ],
                axis=1,
            )
            high, low = split(spectra)
            turned = [
                jnp.concatenate([a, jnp.concatenate([a[:, LANES:], -a[:, :LANES]], axis=1)], axis=0)
                for a in (high, low)
            ]
            both = lax.dot_general(
                jnp.concatenate([high, low], axis=0), turned[0], contract, preferred_element_type=F32
            )
            full = lax.dot_general(high, turned[1], contract, preferred_element_type=F32)
            full = full + both[:rows] + both[rows:]
            packed = jnp.zeros((NB, LANES), F32)
            for i in range(PACK):
                mine = full[i * NB : (i + 1) * NB]
                chosen = jnp.where(upper, mine[:, :LANES], mine[:, LANES:])
                packed = jnp.where(lane // NB == i, chosen, packed)
            out_ref[place] = packed


def packed_grams(first, core, order, outputs, spec):
    count = len(order)
    return pl.pallas_call(
        functools.partial(gram_kernel, order),
        name="gram",
        in_specs=[pl.BlockSpec(memory_space=SMEM)] * 2 + [pl.BlockSpec(memory_space=VMEM)],
        out_specs=[pl.BlockSpec(memory_space=VMEM)] * outputs,
        out_shape=[jax.ShapeDtypeStruct((count, NB, LANES), F32)] * outputs,
        compiler_params=pltpu.CompilerParams(vmem_limit_bytes=24 << 20),
        cost_estimate=pl.CostEstimate(
            flops=outputs * count * 6 * LANES * 4 * LANES * LANES * 2,
            bytes_accessed=outputs * count << 18,
            transcendentals=0,
        ),
    )(first.reshape(1), core.reshape(1), spec)


def unpack_kernel(factor, order_ref, *refs):
    packed_refs, out_ref = refs[:-1], refs[-1]
    row = lax.broadcasted_iota(jnp.int32, (NB, NB), 0)
    column = lax.broadcasted_iota(jnp.int32, (NB, NB), 1)
    for n, packed_ref in enumerate(packed_refs):
        count = packed_ref.shape[0]
        for j in range(count):
            packed = packed_ref[j] * factor
            turned = packed.T
            line = (order_ref[n] * count + j) * PACK
            for i in range(PACK):
                here = packed[:, i * NB : (i + 1) * NB]
                there = turned[i * NB : (i + 1) * NB, :]
                out_ref[0, line + i] = jnp.where(row <= column, here, there)
                out_ref[1, line + i] = jnp.where(
                    row > column, here, jnp.where(row < column, -there, 0.0)
                )


def unpack(parts, order, factor):
    lines = sum(p.shape[0] for p in parts) * PACK
    return pl.pallas_call(
        functools.partial(unpack_kernel, factor),
        name="unpack",
        in_specs=[pl.BlockSpec(memory_space=SMEM)]
        + [pl.BlockSpec(memory_space=VMEM)] * len(parts),
        out_specs=pl.BlockSpec(memory_space=VMEM),
        out_shape=jax.ShapeDtypeStruct((2, lines, NB, NB), F32),
    )(order, *parts)


def swap(value, axis, bits):
    return lax.ppermute(value, axis, [(i, i ^ bits) for i in range(lax.axis_size(axis))])


def exchanged_small(snapshots):
    me = lax.axis_index("tm")
    order = (4, 5, 2, 6, 3, 7, 1)
    rows = snapshots.shape[0]
    pieces = [
        lax.dynamic_slice(snapshots, (0, (me ^ k) * LANES), (rows, LANES)) for k in (*order, 0)
    ]
    pieces = lax.optimization_barrier(pieces)
    pieces = [swap(p, "tm", k) for p, k in zip(pieces, order)] + [pieces[-1]]
    return pieces, jnp.stack([me ^ k for k in (*order, 0)])


def summed_small(spec):
    tm = lax.axis_index("tm")
    core = lax.axis_index("space") % 2
    z, x = tm // 2, tm % 2
    groups = NF // PACK // 4
    order = [(x_ * 4 + i, x_ * 2 + i) for x_ in range(2) for i in range(2)]
    total = None
    for j in (2, 3, 1, 0):
        kept, sent = packed_grams((z ^ j) * groups, core, order, 2, spec)
        part = kept + swap(sent, "space", 1)
        if j:
            part = swap(part, "tm", 2 * j)
        total = part if total is None else total + part
    kept = total.reshape(2, 2, NB, LANES)
    mine = lax.dynamic_index_in_dim(kept, x, 0, keepdims=False)
    other = lax.dynamic_index_in_dim(kept, 1 - x, 0, keepdims=False)
    from_y = swap(mine, "space", 2)
    from_x = swap(other, "tm", 1)
    from_xy = lax.ppermute(
        other,
        ("tm", "space"),
        [(i * 4 + s, (i ^ 1) * 4 + (s ^ 2)) for i in range(8) for s in range(4)],
    )
    mine = mine + from_y + from_x + from_xy
    return [mine, swap(mine, "space", 1)], jnp.stack([core, 1 - core])


def summed_any(spec):
    zero = jnp.int32(0)
    order = [(j, j) for j in range(NF // PACK)]
    (packed,) = packed_grams(zero, zero, order, 1, spec)
    own = lax.psum_scatter(packed, "tm", scatter_dimension=0, tiled=True)
    return [lax.psum(own, "space")], jnp.zeros((1,), jnp.int32)


def body(snapshots, starts, freq_lines):
    groups = lax.axis_size("tm")
    spaces = lax.axis_size("space")
    columns = snapshots.shape[1] // groups
    small = (groups, spaces) == (8, 4)
    if small:
        pieces, where = exchanged_small(snapshots)
    else:
        arranged = snapshots.reshape(snapshots.shape[0], groups, columns)
        series = lax.all_to_all(arranged, "tm", split_axis=1, concat_axis=0, tiled=True)[:, 0, :]
        pieces, where = [series], jnp.zeros((1,), jnp.int32)
    table = spectral_table(freq_lines)
    spec, power_density = block_spectra(starts, table, pieces, where)
    parts, order = summed_small(spec) if small else summed_any(spec)
    return power_density, unpack(parts, order, 1.0 / (NB * columns * groups * spaces))


def solution(mesh):
    placed = (P("tm", "space"), P(), P())
    return jax.shard_map(
        body,
        mesh=mesh,
        in_specs=placed,
        out_specs=(P(None, ("space", "tm")), P(None, "tm", None, None)),
        check_vma=False,
    )
```

```python
import functools
import math

import jax
import jax.numpy as jnp
from jax import lax
from jax.experimental import pallas as pl
from jax.experimental.pallas import tpu as pltpu
from jax.sharding import PartitionSpec as P

NFFT = 256
NF = 128
NB = 32
LANES = 128
PACK = LANES // NB
PITCH = NB + 8
LAST = 2
LATE = 12
CORE_STEP = 2
F32 = jnp.float32
BF16 = jnp.bfloat16
VMEM = pltpu.VMEM
SMEM = pltpu.SMEM


def spectral_table(freq_lines):
    moments = jnp.arange(NFFT, dtype=jnp.int32)
    cycle = freq_lines[:, None] * moments[None, :] % NFFT
    angles = 2.0 * math.pi / NFFT * cycle.astype(jnp.float32)
    window = 0.5 - 0.5 * jnp.cos(2.0 * math.pi / NFFT * moments.astype(jnp.float32))
    window = window / jnp.sqrt(jnp.sum(window * window))
    return jnp.concatenate(
        [window[None, :] * jnp.cos(angles), -window[None, :] * jnp.sin(angles)], axis=0
    )


def split(x):
    high = x.astype(BF16)
    return high, (x - high.astype(F32)).astype(BF16)


def transform(halves, series, starts_ref, numbers, spec_ref):
    block = jnp.concatenate([series[pl.ds(starts_ref[b], NFFT), :] for b in numbers], axis=1)
    x_high, x_low = split(block)
    both = jnp.dot(halves[...], x_high, preferred_element_type=F32)
    out = jnp.dot(halves[:NFFT], x_low, preferred_element_type=F32)
    out = out + both[:NFFT] + both[NFFT:]
    power = []
    for i, b in enumerate(numbers):
        part = out[:, i * LANES : (i + 1) * LANES]
        spec_ref[pl.ds(b, 2 * NF, stride=PITCH), :] = part
        square = part * part
        power.append(square[:NF] + square[NF:])
    return (power[0] + power[1]) * (1.0 / NB)


def split_table(table_ref, halves):
    high, low = split(table_ref[...])
    halves[:NFFT] = high
    halves[NFFT:] = low


def gram(rows_of, line):
    rows = PACK * NB
    row = lax.broadcasted_iota(jnp.int32, (rows, LANES), 0) % NB
    lane = lax.broadcasted_iota(jnp.int32, (rows, LANES), 1)
    spectra = jnp.concatenate(
        [
            jnp.concatenate([rows_of(part, line + i) for i in range(PACK)], axis=0)
            for part in range(2)
        ],
        axis=1,
    )
    high, low = split(spectra)
    turned = jnp.concatenate([high[:, LANES:], -high[:, :LANES]], axis=1)
    both = lax.dot_general(
        jnp.concatenate([high, low], axis=0),
        jnp.concatenate([high, turned], axis=0),
        (((1,), (1,)), ((), ())),
        preferred_element_type=F32,
    )
    cross = both[rows:]
    mirrored = jnp.where(row >= lane % NB, cross[:, :LANES], -cross[:, LANES:])
    full = both[:rows] + cross
    full = jnp.where(row <= lane % NB, full[:, :LANES], full[:, LANES:]) + mirrored.T
    packed = full[:NB]
    for i in range(1, PACK):
        packed = jnp.where(lane[:NB] // NB == i, full[i * NB : (i + 1) * NB], packed)
    return packed


def line_rows(spec_ref, part, line):
    return spec_ref[pl.ds(pl.multiple_of((part * NF + line) * PITCH, 8), NB), :]


def cut_kernel(order, snapshots_ref, *refs):
    me = lax.axis_index("tm")
    pieces, sems = refs[:-1], refs[-1]
    copies = [
        pltpu.make_async_copy(
            snapshots_ref.at[:, pl.ds(pl.multiple_of((me ^ k) * LANES, LANES), LANES)],
            piece,
            sems.at[i],
        )
        for i, (k, piece) in enumerate(zip(order, pieces))
    ]
    for copy in copies:
        copy.start()
    for copy in copies:
        copy.wait()


def cut(order, snapshots):
    rows = snapshots.shape[0]
    return pl.pallas_call(
        functools.partial(cut_kernel, order),
        name="cut",
        in_specs=[pl.BlockSpec(memory_space=pltpu.HBM)],
        out_specs=[pl.BlockSpec(memory_space=VMEM)] * len(order),
        out_shape=[jax.ShapeDtypeStruct((rows, LANES), F32)] * len(order),
        scratch_shapes=[pltpu.SemaphoreType.DMA((len(order),))],
        compiler_params=pltpu.CompilerParams(vmem_limit_bytes=8 << 20),
    )(snapshots)


def early_kernel(rows, base_ref, where_ref, starts_ref, table_ref, *refs):
    pieces, (series, spec_ref, power_ref, halves) = refs[:-4], refs[-4:]
    for k, piece in enumerate(pieces):
        series[pl.ds(pl.multiple_of(where_ref[k] * rows, 8), rows), :] = piece[...]
    split_table(table_ref, halves)
    power_ref[...] = jnp.zeros_like(power_ref)

    def step(pair, carry):
        numbers = [2 * pair + i for i in range(2)]
        numbers = [jnp.where(b < base_ref[0], b, b + LATE) for b in numbers]
        power_ref[...] += transform(halves, series, starts_ref, numbers, spec_ref)
        return carry

    lax.fori_loop(0, (NB - LATE) // 2, step, 0, unroll=5)


def early(base, where, starts, table, pieces):
    rows = pieces[0].shape[0]
    smem, vmem = pl.BlockSpec(memory_space=SMEM), pl.BlockSpec(memory_space=VMEM)
    return pl.pallas_call(
        functools.partial(early_kernel, rows),
        name="early",
        in_specs=[smem] * 3 + [vmem] * (1 + len(pieces)),
        out_specs=[vmem] * 4,
        out_shape=[
            jax.ShapeDtypeStruct(((len(pieces) + LAST) * rows, LANES), F32),
            jax.ShapeDtypeStruct((2 * NF * PITCH, LANES), F32),
            jax.ShapeDtypeStruct((NF, LANES), F32),
            jax.ShapeDtypeStruct((2 * NFFT, NFFT), BF16),
        ],
        compiler_params=pltpu.CompilerParams(vmem_limit_bytes=20 << 20),
        cost_estimate=pl.CostEstimate(
            flops=6 * 2 * NF * NFFT * (NB - LATE) * LANES, bytes_accessed=4 << 20, transcendentals=0
        ),
    )(base, where, starts, table, *pieces)


def late_kernel(
    base_ref, where_ref, core_ref, firsts_ref, starts_ref,
    halves, series_ref, spec_ref, early_power_ref, *refs,
):
    pieces, (power_ref, sent_ref) = refs[:LAST], refs[LAST : LAST + 2]
    kept_refs, (series, late_spec) = refs[LAST + 2 : -2], refs[-2:]
    rows, base = pieces[0].shape[0], base_ref[0]
    series[...] = series_ref[...]
    for k, piece in enumerate(pieces):
        series[pl.ds(pl.multiple_of(where_ref[k] * rows, 8), rows), :] = piece[...]
    power = early_power_ref[...]
    for pair in range(LATE // 2):
        numbers = [base + 2 * pair + i for i in range(2)]
        power = power + transform(halves, series, starts_ref, numbers, late_spec)
    power_ref[...] = power
    block = lax.broadcasted_iota(jnp.int32, (NB, LANES), 0)
    is_late = (block >= base) & (block < base + LATE)

    def rows_of(part, line):
        return jnp.where(
            is_late, line_rows(late_spec, part, line), line_rows(spec_ref, part, line)
        )

    core = core_ref[0]
    half = len(kept_refs)
    for n, kept_ref in enumerate(kept_refs):
        for i in range(half):
            group = firsts_ref[n] + (i // CORE_STEP) * 2 * CORE_STEP + i % CORE_STEP
            kept_ref[i] = gram(rows_of, (group + core * CORE_STEP) * PACK)
            sent_ref[n * half + i] = gram(rows_of, (group + (1 - core) * CORE_STEP) * PACK)


def late(base, where, core, firsts, starts, halves, series, spec, power, pieces):
    quarters = firsts.shape[0]
    half = NF // PACK // quarters // 2
    smem, vmem = pl.BlockSpec(memory_space=SMEM), pl.BlockSpec(memory_space=VMEM)
    return pl.pallas_call(
        late_kernel,
        name="late",
        in_specs=[smem] * 5 + [vmem] * (4 + len(pieces)),
        out_specs=[vmem] * (2 + quarters),
        out_shape=[
            jax.ShapeDtypeStruct((NF, LANES), F32),
            jax.ShapeDtypeStruct((quarters * half, NB, LANES), F32),
        ]
        + [jax.ShapeDtypeStruct((half, NB, LANES), F32)] * quarters,
        scratch_shapes=[VMEM(series.shape, F32), VMEM(spec.shape, F32)],
        compiler_params=pltpu.CompilerParams(vmem_limit_bytes=28 << 20),
        cost_estimate=pl.CostEstimate(
            flops=NF // PACK * 6 * LANES * 4 * LANES * LANES * 2,
            bytes_accessed=8 << 20,
            transcendentals=0,
        ),
    )(base, where, core, firsts, starts, halves, series, spec, power, *pieces)


def whole_kernel(starts_ref, table_ref, series_ref, power_ref, packed_ref, halves, spec):
    split_table(table_ref, halves)
    power_ref[...] = jnp.zeros_like(power_ref)

    def step(pair, carry):
        numbers = [2 * pair + i for i in range(2)]
        power_ref[...] += transform(halves, series_ref, starts_ref, numbers, spec)
        return carry

    lax.fori_loop(0, NB // 2, step, 0, unroll=4)

    def step_gram(group, carry):
        packed_ref[group] = gram(functools.partial(line_rows, spec), group * PACK)
        return carry

    lax.fori_loop(0, NF // PACK, step_gram, 0, unroll=8)


def whole(starts, table, series):
    smem, vmem = pl.BlockSpec(memory_space=SMEM), pl.BlockSpec(memory_space=VMEM)
    return pl.pallas_call(
        whole_kernel,
        name="whole",
        in_specs=[smem, vmem, vmem],
        out_specs=[vmem] * 2,
        out_shape=[
            jax.ShapeDtypeStruct((NF, LANES), F32),
            jax.ShapeDtypeStruct((NF // PACK, NB, LANES), F32),
        ],
        scratch_shapes=[VMEM((2 * NFFT, NFFT), BF16), VMEM((2 * NF * PITCH, LANES), F32)],
        compiler_params=pltpu.CompilerParams(vmem_limit_bytes=28 << 20),
    )(starts, table, series)


def unpack_kernel(factor, order_ref, *refs):
    packed_refs, out_ref = refs[:-1], refs[-1]
    row = lax.broadcasted_iota(jnp.int32, (NB, NB), 0)
    column = lax.broadcasted_iota(jnp.int32, (NB, NB), 1)
    for n, packed_ref in enumerate(packed_refs):
        count = packed_ref.shape[0]
        for j in range(count):
            packed = packed_ref[j] * factor
            turned = packed.T
            line = (order_ref[n] * count + j) * PACK
            for i in range(PACK):
                here = packed[:, i * NB : (i + 1) * NB]
                there = turned[i * NB : (i + 1) * NB, :]
                out_ref[0, line + i] = jnp.where(row <= column, here, there)
                out_ref[1, line + i] = jnp.where(
                    row > column, here, jnp.where(row < column, -there, 0.0)
                )


def unpack(parts, order, factor):
    lines = sum(p.shape[0] for p in parts) * PACK
    return pl.pallas_call(
        functools.partial(unpack_kernel, factor),
        name="unpack",
        in_specs=[pl.BlockSpec(memory_space=SMEM)]
        + [pl.BlockSpec(memory_space=VMEM)] * len(parts),
        out_specs=pl.BlockSpec(memory_space=VMEM),
        out_shape=jax.ShapeDtypeStruct((2, lines, NB, NB), F32),
        compiler_params=pltpu.CompilerParams(vmem_limit_bytes=8 << 20),
    )(order, *parts)


def swap(value, axis, bits):
    return lax.ppermute(value, axis, [(i, i ^ bits) for i in range(lax.axis_size(axis))])


def spread_small(snapshots, starts, table):
    me = lax.axis_index("tm")
    core = lax.axis_index("space") % 2
    z, x = me // 2, me % 2
    order = (4, 2, 1, 5, 3, 6, 7)
    rows = snapshots.shape[0]
    *pieces, own = cut((*order, 0), snapshots)
    pieces = [swap(p, "tm", k) for p, k in zip(pieces, order)]
    pieces, last = pieces[:-LAST] + [own], pieces[-LAST:]
    where = jnp.stack([me ^ k for k in (*order[:-LAST], 0)])
    before = jnp.sum((starts + (NFFT - 1) < (z ^ 3) * LAST * rows).astype(jnp.int32))
    base = jnp.minimum(before, NB - LATE).reshape(1)
    series, spec, power, halves = early(base, where, starts, table, pieces)
    groups = NF // PACK // 4
    away = (2, 1, 3)
    firsts = jnp.stack([(z ^ j) * groups for j in (*away, 0)])
    power, sent, *kept = late(
        base, jnp.stack([me ^ k for k in order[-LAST:]]), core.reshape(1), firsts, starts,
        halves, series, spec, power, last,
    )
    theirs = swap(sent, "space", 1)
    half = groups // 2
    terms = [k + theirs[n * half : (n + 1) * half] for n, k in enumerate(kept)]
    terms = [swap(t, "tm", 2 * j) for j, t in zip(away, terms)] + terms[-1:]
    lower, upper = (sum(t[i * half // 2 : (i + 1) * half // 2] for t in terms) for i in range(2))
    mine, other = jnp.where(x == 0, lower, upper), jnp.where(x == 0, upper, lower)
    from_y = swap(mine, "space", 2)
    from_x = swap(other, "tm", 1)
    from_xy = lax.ppermute(
        other,
        ("tm", "space"),
        [(i * 4 + s, (i ^ 1) * 4 + (s ^ 2)) for i in range(8) for s in range(4)],
    )
    mine = mine + from_y + from_x + from_xy
    return power, [mine, swap(mine, "space", 1)], jnp.stack([core, 1 - core])


def spread_any(snapshots, starts, table):
    groups = lax.axis_size("tm")
    arranged = snapshots.reshape(snapshots.shape[0], groups, -1)
    series = lax.all_to_all(arranged, "tm", split_axis=1, concat_axis=0, tiled=True)[:, 0, :]
    power, packed = whole(starts, table, series)
    own = lax.psum_scatter(packed, "tm", scatter_dimension=0, tiled=True)
    return power, [lax.psum(own, "space")], jnp.zeros((1,), jnp.int32)


def body(snapshots, starts, freq_lines):
    groups = lax.axis_size("tm")
    spaces = lax.axis_size("space")
    table = spectral_table(freq_lines)
    spread = spread_small if (groups, spaces) == (8, 4) else spread_any
    power_density, parts, order = spread(snapshots, starts, table)
    return power_density, unpack(parts, order, 1.0 / (NB * snapshots.shape[1] * spaces))


def solution(mesh):
    placed = (P("tm", "space"), P(), P())
    return jax.shard_map(
        body,
        mesh=mesh,
        in_specs=placed,
        out_specs=(P(None, ("space", "tm")), P(None, "tm", None, None)),
        check_vma=False,
    )
```

```python
import functools
import math

import jax
import jax.numpy as jnp
from jax import lax
from jax.experimental import pallas as pl
from jax.experimental.pallas import tpu as pltpu
from jax.sharding import PartitionSpec as P

NFFT = 256
NF = 128
NB = 32
LANES = 128
PACK = LANES // NB
PITCH = NB + 8
LATE = 8
WINDOW = (LATE - 1) * NFFT // 2 + NFFT // 2 + NFFT + 8
CORE_STEP = 2
F32 = jnp.float32
BF16 = jnp.bfloat16
VMEM = pltpu.VMEM
SMEM = pltpu.SMEM


def spectral_table(freq_lines):
    moments = jnp.arange(NFFT, dtype=jnp.int32)
    cycle = freq_lines[:, None] * moments[None, :] % NFFT
    angles = 2.0 * math.pi / NFFT * cycle.astype(jnp.float32)
    window = 0.5 - 0.5 * jnp.cos(2.0 * math.pi / NFFT * moments.astype(jnp.float32))
    window = window / jnp.sqrt(jnp.sum(window * window))
    return jnp.concatenate(
        [window[None, :] * jnp.cos(angles), -window[None, :] * jnp.sin(angles)], axis=0
    )


def split(x):
    high = x.astype(BF16)
    return high, (x - high.astype(F32)).astype(BF16)


def transform(halves, blocks, numbers, spec_ref):
    x_high, x_low = split(jnp.concatenate(blocks, axis=1))
    both = jnp.dot(halves[...], x_high, preferred_element_type=F32)
    out = jnp.dot(halves[:NFFT], x_low, preferred_element_type=F32)
    out = out + both[:NFFT] + both[NFFT:]
    power = []
    for i, b in enumerate(numbers):
        part = out[:, i * LANES : (i + 1) * LANES]
        spec_ref[pl.ds(b, 2 * NF, stride=PITCH), :] = part
        square = part * part
        power.append(square[:NF] + square[NF:])
    return (power[0] + power[1]) * (1.0 / NB)


def split_table(table_ref, halves):
    high, low = split(table_ref[...])
    halves[:NFFT] = high
    halves[NFFT:] = low


def gram(rows_of, line):
    rows = PACK * NB
    row = lax.broadcasted_iota(jnp.int32, (rows, LANES), 0) % NB
    lane = lax.broadcasted_iota(jnp.int32, (rows, LANES), 1)
    spectra = jnp.concatenate(
        [
            jnp.concatenate([rows_of(part, line + i) for i in range(PACK)], axis=0)
            for part in range(2)
        ],
        axis=1,
    )
    high, low = split(spectra)
    turned = jnp.concatenate([high[:, LANES:], -high[:, :LANES]], axis=1)
    both = lax.dot_general(
        jnp.concatenate([high, low], axis=0),
        jnp.concatenate([high, turned], axis=0),
        (((1,), (1,)), ((), ())),
        preferred_element_type=F32,
    )
    cross = both[rows:]
    mirrored = jnp.where(row >= lane % NB, cross[:, :LANES], -cross[:, LANES:])
    full = both[:rows] + cross
    full = jnp.where(row <= lane % NB, full[:, :LANES], full[:, LANES:]) + mirrored.T
    packed = full[:NB]
    for i in range(1, PACK):
        packed = jnp.where(lane[:NB] // NB == i, full[i * NB : (i + 1) * NB], packed)
    return packed


def line_rows(spec_ref, part, line):
    return spec_ref[pl.ds(pl.multiple_of((part * NF + line) * PITCH, 8), NB), :]


def cut_kernel(order, snapshots_ref, *refs):
    me = lax.axis_index("tm")
    pieces, sems = refs[:-1], refs[-1]
    copies = [
        pltpu.make_async_copy(
            snapshots_ref.at[:, pl.ds(pl.multiple_of((me ^ k) * LANES, LANES), LANES)],
            piece,
            sems.at[i],
        )
        for i, (k, piece) in enumerate(zip(order, pieces))
    ]
    for copy in copies:
        copy.start()
    for copy in copies:
        copy.wait()


def cut(order, snapshots):
    rows = snapshots.shape[0]
    return pl.pallas_call(
        functools.partial(cut_kernel, order),
        name="cut",
        in_specs=[pl.BlockSpec(memory_space=pltpu.HBM)],
        out_specs=[pl.BlockSpec(memory_space=VMEM)] * len(order),
        out_shape=[jax.ShapeDtypeStruct((rows, LANES), F32)] * len(order),
        scratch_shapes=[pltpu.SemaphoreType.DMA((len(order),))],
        compiler_params=pltpu.CompilerParams(vmem_limit_bytes=8 << 20),
    )(snapshots)


def early_kernel(rows, base_ref, corner_ref, where_ref, starts_ref, table_ref, *refs):
    pieces, (window_ref, spec_ref, power_ref, halves, series) = refs[:-5], refs[-5:]
    for k, piece in enumerate(pieces):
        series[pl.ds(pl.multiple_of(where_ref[k] * rows, 8), rows), :] = piece[...]
    window_ref[...] = series[pl.ds(pl.multiple_of(corner_ref[0], 8), WINDOW), :]
    split_table(table_ref, halves)
    power_ref[...] = jnp.zeros_like(power_ref)

    def step(pair, carry):
        numbers = [2 * pair + i for i in range(2)]
        numbers = [jnp.where(b < base_ref[0], b, b + LATE) for b in numbers]
        blocks = [series[pl.ds(starts_ref[b], NFFT), :] for b in numbers]
        power_ref[...] += transform(halves, blocks, numbers, spec_ref)
        return carry

    lax.fori_loop(0, (NB - LATE) // 2, step, 0, unroll=4)


def early(base, corner, where, starts, table, pieces):
    rows = pieces[0].shape[0]
    smem, vmem = pl.BlockSpec(memory_space=SMEM), pl.BlockSpec(memory_space=VMEM)
    return pl.pallas_call(
        functools.partial(early_kernel, rows),
        name="early",
        in_specs=[smem] * 4 + [vmem] * (1 + len(pieces)),
        out_specs=[vmem] * 4,
        out_shape=[
            jax.ShapeDtypeStruct((WINDOW, LANES), F32),
            jax.ShapeDtypeStruct((2 * NF * PITCH, LANES), F32),
            jax.ShapeDtypeStruct((NF, LANES), F32),
            jax.ShapeDtypeStruct((2 * NFFT, NFFT), BF16),
        ],
        scratch_shapes=[VMEM(((len(pieces) + 1) * rows, LANES), F32)],
        compiler_params=pltpu.CompilerParams(vmem_limit_bytes=20 << 20),
        cost_estimate=pl.CostEstimate(
            flops=6 * 2 * NF * NFFT * (NB - LATE) * LANES, bytes_accessed=4 << 20, transcendentals=0
        ),
    )(base, corner, where, starts, table, *pieces)


def late_kernel(
    base_ref, corner_ref, where_ref, core_ref, firsts_ref, starts_ref,
    halves, window_ref, spec_ref, early_power_ref, piece_ref, power_ref, sent_ref, *refs,
):
    kept_refs, (series, late_spec) = refs[:-2], refs[-2:]
    rows, base = piece_ref.shape[0], base_ref[0]
    origin = corner_ref[0] - rows
    series[pl.ds(rows, WINDOW), :] = window_ref[...]
    series[pl.ds(pl.multiple_of(where_ref[0] * rows - origin, 8), rows), :] = piece_ref[...]
    power = early_power_ref[...]
    for pair in range(LATE // 2):
        numbers = [base + 2 * pair + i for i in range(2)]
        blocks = [series[pl.ds(starts_ref[b] - origin, NFFT), :] for b in numbers]
        power = power + transform(halves, blocks, numbers, late_spec)
    power_ref[...] = power
    block = lax.broadcasted_iota(jnp.int32, (NB, LANES), 0)
    is_late = (block >= base) & (block < base + LATE)

    def rows_of(part, line):
        return jnp.where(
            is_late, line_rows(late_spec, part, line), line_rows(spec_ref, part, line)
        )

    core = core_ref[0]
    half = len(kept_refs)
    for n, kept_ref in enumerate(kept_refs):
        for i in range(half):
            group = firsts_ref[n] + (i // CORE_STEP) * 2 * CORE_STEP + i % CORE_STEP
            kept_ref[i] = gram(rows_of, (group + core * CORE_STEP) * PACK)
            sent_ref[n * half + i] = gram(rows_of, (group + (1 - core) * CORE_STEP) * PACK)


def late(base, corner, where, core, firsts, starts, halves, window, spec, power, piece):
    quarters = firsts.shape[0]
    half = NF // PACK // quarters // 2
    smem, vmem = pl.BlockSpec(memory_space=SMEM), pl.BlockSpec(memory_space=VMEM)
    return pl.pallas_call(
        late_kernel,
        name="late",
        in_specs=[smem] * 6 + [vmem] * 5,
        out_specs=[vmem] * (2 + quarters),
        out_shape=[
            jax.ShapeDtypeStruct((NF, LANES), F32),
            jax.ShapeDtypeStruct((quarters * half, NB, LANES), F32),
        ]
        + [jax.ShapeDtypeStruct((half, NB, LANES), F32)] * quarters,
        scratch_shapes=[VMEM((2 * piece.shape[0] + WINDOW, LANES), F32), VMEM(spec.shape, F32)],
        compiler_params=pltpu.CompilerParams(vmem_limit_bytes=28 << 20),
        cost_estimate=pl.CostEstimate(
            flops=NF // PACK * 6 * LANES * 4 * LANES * LANES * 2,
            bytes_accessed=8 << 20,
            transcendentals=0,
        ),
    )(base, corner, where, core, firsts, starts, halves, window, spec, power, piece)


def whole_kernel(starts_ref, table_ref, series_ref, power_ref, packed_ref, halves, spec):
    split_table(table_ref, halves)
    power_ref[...] = jnp.zeros_like(power_ref)

    def step(pair, carry):
        numbers = [2 * pair + i for i in range(2)]
        blocks = [series_ref[pl.ds(starts_ref[b], NFFT), :] for b in numbers]
        power_ref[...] += transform(halves, blocks, numbers, spec)
        return carry

    lax.fori_loop(0, NB // 2, step, 0, unroll=4)

    def step_gram(group, carry):
        packed_ref[group] = gram(functools.partial(line_rows, spec), group * PACK)
        return carry

    lax.fori_loop(0, NF // PACK, step_gram, 0, unroll=8)


def whole(starts, table, series):
    smem, vmem = pl.BlockSpec(memory_space=SMEM), pl.BlockSpec(memory_space=VMEM)
    return pl.pallas_call(
        whole_kernel,
        name="whole",
        in_specs=[smem, vmem, vmem],
        out_specs=[vmem] * 2,
        out_shape=[
            jax.ShapeDtypeStruct((NF, LANES), F32),
            jax.ShapeDtypeStruct((NF // PACK, NB, LANES), F32),
        ],
        scratch_shapes=[VMEM((2 * NFFT, NFFT), BF16), VMEM((2 * NF * PITCH, LANES), F32)],
        compiler_params=pltpu.CompilerParams(vmem_limit_bytes=28 << 20),
    )(starts, table, series)


def unpack_kernel(factor, order_ref, packed_ref, *refs):
    out_ref, matrices, sem = refs[-3:]
    row = lax.broadcasted_iota(jnp.int32, (NB, NB), 0)
    column = lax.broadcasted_iota(jnp.int32, (NB, NB), 1)
    count = packed_ref.shape[0]
    for j in range(count):
        packed = packed_ref[j] * factor
        turned = packed.T
        for i in range(PACK):
            here = packed[:, i * NB : (i + 1) * NB]
            there = turned[i * NB : (i + 1) * NB, :]
            matrices[0, j * PACK + i] = jnp.where(row <= column, here, there)
            matrices[1, j * PACK + i] = jnp.where(
                row > column, here, jnp.where(row < column, -there, 0.0)
            )
    lines = count * PACK
    copy = pltpu.make_async_copy(
        matrices, out_ref.at[:, pl.ds(order_ref[0] * lines, lines)], sem
    )
    copy.start()
    copy.wait()


def unpack(parts, order, factor):
    lines = parts[0].shape[0] * PACK
    out = []
    for n, part in enumerate(parts):
        out = [
            pl.pallas_call(
                functools.partial(unpack_kernel, factor),
                name="unpack",
                in_specs=[pl.BlockSpec(memory_space=SMEM), pl.BlockSpec(memory_space=VMEM)]
                + [pl.BlockSpec(memory_space=pl.ANY)] * len(out),
                out_specs=pl.BlockSpec(memory_space=pl.ANY),
                out_shape=jax.ShapeDtypeStruct((2, len(parts) * lines, NB, NB), F32),
                input_output_aliases={2: 0} if out else {},
                scratch_shapes=[VMEM((2, lines, NB, NB), F32), pltpu.SemaphoreType.DMA],
                compiler_params=pltpu.CompilerParams(vmem_limit_bytes=8 << 20),
            )(order[n].reshape(1), part, *out)
        ]
    return out[0]


def swap(value, axis, bits):
    return lax.ppermute(value, axis, [(i, i ^ bits) for i in range(lax.axis_size(axis))])


def spread_small(snapshots, starts, table):
    me = lax.axis_index("tm")
    core = lax.axis_index("space") % 2
    z, x = me // 2, me % 2
    order = (4, 2, 1, 5, 3, 6, 7)
    rows = snapshots.shape[0]
    *pieces, own = cut((*order, 0), snapshots)
    pieces = [swap(p, "tm", k) for p, k in zip(pieces, order)]
    pieces, last = pieces[:-1] + [own], pieces[-1]
    where = jnp.stack([me ^ k for k in (*order[:-1], 0)])
    late_part = me ^ order[-1]
    before = jnp.sum((starts + (NFFT - 1) < late_part * rows).astype(jnp.int32))
    base = jnp.minimum(before, NB - LATE)
    corner = jnp.minimum(starts[base] // 8 * 8, lax.axis_size("tm") * rows - WINDOW).reshape(1)
    base = base.reshape(1)
    window, spec, power, halves = early(base, corner, where, starts, table, pieces)
    groups = NF // PACK // 4
    away = (2, 1, 3)
    firsts = jnp.stack([(z ^ j) * groups for j in (*away, 0)])
    power, sent, *kept = late(
        base, corner, late_part.reshape(1), core.reshape(1), firsts, starts,
        halves, window, spec, power, last,
    )
    theirs = swap(sent, "space", 1)
    half = groups // 2
    terms = [k + theirs[n * half : (n + 1) * half] for n, k in enumerate(kept)]
    terms = [swap(t, "tm", 2 * j) for j, t in zip(away, terms)] + terms[-1:]
    lower, upper = (sum(t[i * half // 2 : (i + 1) * half // 2] for t in terms) for i in range(2))
    mine, other = jnp.where(x == 0, lower, upper), jnp.where(x == 0, upper, lower)
    from_y = swap(mine, "space", 2)
    from_x = swap(other, "tm", 1)
    from_xy = lax.ppermute(
        other,
        ("tm", "space"),
        [(i * 4 + s, (i ^ 1) * 4 + (s ^ 2)) for i in range(8) for s in range(4)],
    )
    mine = mine + from_y + from_x + from_xy
    return power, [mine, swap(mine, "space", 1)], [core, 1 - core]


def spread_any(snapshots, starts, table):
    groups = lax.axis_size("tm")
    arranged = snapshots.reshape(snapshots.shape[0], groups, -1)
    series = lax.all_to_all(arranged, "tm", split_axis=1, concat_axis=0, tiled=True)[:, 0, :]
    power, packed = whole(starts, table, series)
    own = lax.psum_scatter(packed, "tm", scatter_dimension=0, tiled=True)
    return power, [lax.psum(own, "space")], [jnp.int32(0)]


def body(snapshots, starts, freq_lines):
    groups = lax.axis_size("tm")
    spaces = lax.axis_size("space")
    table = spectral_table(freq_lines)
    spread = spread_small if (groups, spaces) == (8, 4) else spread_any
    power_density, parts, order = spread(snapshots, starts, table)
    return power_density, unpack(parts, order, 1.0 / (NB * snapshots.shape[1] * spaces))


def solution(mesh):
    placed = (P("tm", "space"), P(), P())
    return jax.shard_map(
        body,
        mesh=mesh,
        in_specs=placed,
        out_specs=(P(None, ("space", "tm")), P(None, "tm", None, None)),
        check_vma=False,
    )
```

```python
import functools
import math

import jax
import jax.numpy as jnp
from jax import lax
from jax.experimental import pallas as pl
from jax.experimental.pallas import tpu as pltpu
from jax.sharding import PartitionSpec as P

NFFT = 256
NF = 128
NB = 32
LANES = 128
PACK = LANES // NB
PITCH = NB + 8
LATE = 8
WINDOW = (LATE - 1) * NFFT // 2 + NFFT // 2 + NFFT + 8
CORE_STEP = 2
F32 = jnp.float32
BF16 = jnp.bfloat16
VMEM = pltpu.VMEM
SMEM = pltpu.SMEM


def spectral_table(freq_lines):
    moments = jnp.arange(NFFT, dtype=jnp.int32)
    cycle = freq_lines[:, None] * moments[None, :] % NFFT
    angles = 2.0 * math.pi / NFFT * cycle.astype(jnp.float32)
    window = 0.5 - 0.5 * jnp.cos(2.0 * math.pi / NFFT * moments.astype(jnp.float32))
    window = window / jnp.sqrt(jnp.sum(window * window))
    return jnp.concatenate(
        [window[None, :] * jnp.cos(angles), -window[None, :] * jnp.sin(angles)], axis=0
    )


def split(x):
    high = x.astype(BF16)
    return high, (x - high.astype(F32)).astype(BF16)


def transform(halves, blocks, numbers, spec_ref):
    x_high, x_low = split(jnp.concatenate(blocks, axis=1))
    both = jnp.dot(halves[...], x_high, preferred_element_type=F32)
    out = jnp.dot(halves[:NFFT], x_low, preferred_element_type=F32)
    out = out + both[:NFFT] + both[NFFT:]
    power = []
    for i, b in enumerate(numbers):
        part = out[:, i * LANES : (i + 1) * LANES]
        spec_ref[pl.ds(b, 2 * NF, stride=PITCH), :] = part
        square = part * part
        power.append(square[:NF] + square[NF:])
    return (power[0] + power[1]) * (1.0 / NB)


def split_table(table_ref, halves):
    high, low = split(table_ref[...])
    halves[:NFFT] = high
    halves[NFFT:] = low


def gram(rows_of, line):
    rows = PACK * NB
    row = lax.broadcasted_iota(jnp.int32, (rows, LANES), 0) % NB
    lane = lax.broadcasted_iota(jnp.int32, (rows, LANES), 1)
    spectra = jnp.concatenate(
        [
            jnp.concatenate([rows_of(part, line + i) for i in range(PACK)], axis=0)
            for part in range(2)
        ],
        axis=1,
    )
    high, low = split(spectra)
    turned = jnp.concatenate([high[:, LANES:], -high[:, :LANES]], axis=1)
    both = lax.dot_general(
        jnp.concatenate([high, low], axis=0),
        jnp.concatenate([high, turned], axis=0),
        (((1,), (1,)), ((), ())),
        preferred_element_type=F32,
    )
    cross = both[rows:]
    mirrored = jnp.where(row >= lane % NB, cross[:, :LANES], -cross[:, LANES:])
    full = both[:rows] + cross
    full = jnp.where(row <= lane % NB, full[:, :LANES], full[:, LANES:]) + mirrored.T
    packed = full[:NB]
    for i in range(1, PACK):
        packed = jnp.where(lane[:NB] // NB == i, full[i * NB : (i + 1) * NB], packed)
    return packed


def line_rows(spec_ref, part, line):
    return spec_ref[pl.ds(pl.multiple_of((part * NF + line) * PITCH, 8), NB), :]


def cut_kernel(order, snapshots_ref, *refs):
    me = lax.axis_index("tm")
    pieces, sems = refs[:-1], refs[-1]
    copies = [
        pltpu.make_async_copy(
            snapshots_ref.at[:, pl.ds(pl.multiple_of((me ^ k) * LANES, LANES), LANES)],
            piece,
            sems.at[i],
        )
        for i, (k, piece) in enumerate(zip(order, pieces))
    ]
    for copy in copies:
        copy.start()
    for copy in copies:
        copy.wait()


def cut(order, snapshots):
    rows = snapshots.shape[0]
    return pl.pallas_call(
        functools.partial(cut_kernel, order),
        name="cut",
        in_specs=[pl.BlockSpec(memory_space=pltpu.HBM)],
        out_specs=[pl.BlockSpec(memory_space=VMEM)] * len(order),
        out_shape=[jax.ShapeDtypeStruct((rows, LANES), F32)] * len(order),
        scratch_shapes=[pltpu.SemaphoreType.DMA((len(order),))],
        compiler_params=pltpu.CompilerParams(vmem_limit_bytes=8 << 20),
    )(snapshots)


def early_kernel(rows, base_ref, corner_ref, where_ref, starts_ref, table_ref, *refs):
    pieces, (window_ref, spec_ref, power_ref, halves, series) = refs[:-5], refs[-5:]
    for k, piece in enumerate(pieces):
        series[pl.ds(pl.multiple_of(where_ref[k] * rows, 8), rows), :] = piece[...]
    window_ref[...] = series[pl.ds(pl.multiple_of(corner_ref[0], 8), WINDOW), :]
    split_table(table_ref, halves)
    power_ref[...] = jnp.zeros_like(power_ref)

    def step(pair, carry):
        numbers = [2 * pair + i for i in range(2)]
        numbers = [jnp.where(b < base_ref[0], b, b + LATE) for b in numbers]
        blocks = [series[pl.ds(starts_ref[b], NFFT), :] for b in numbers]
        power_ref[...] += transform(halves, blocks, numbers, spec_ref)
        return carry

    lax.fori_loop(0, (NB - LATE) // 2, step, 0, unroll=4)


def early(base, corner, where, starts, table, pieces):
    rows = pieces[0].shape[0]
    smem, vmem = pl.BlockSpec(memory_space=SMEM), pl.BlockSpec(memory_space=VMEM)
    return pl.pallas_call(
        functools.partial(early_kernel, rows),
        name="early",
        in_specs=[smem] * 4 + [vmem] * (1 + len(pieces)),
        out_specs=[vmem] * 4,
        out_shape=[
            jax.ShapeDtypeStruct((WINDOW, LANES), F32),
            jax.ShapeDtypeStruct((2 * NF * PITCH, LANES), F32),
            jax.ShapeDtypeStruct((NF, LANES), F32),
            jax.ShapeDtypeStruct((2 * NFFT, NFFT), BF16),
        ],
        scratch_shapes=[VMEM(((len(pieces) + 1) * rows, LANES), F32)],
        compiler_params=pltpu.CompilerParams(vmem_limit_bytes=20 << 20),
        cost_estimate=pl.CostEstimate(
            flops=6 * 2 * NF * NFFT * (NB - LATE) * LANES, bytes_accessed=4 << 20, transcendentals=0
        ),
    )(base, corner, where, starts, table, *pieces)


def packed_quarters(base, core, firsts_ref, spec_ref, late_spec, sent_ref, kept_refs):
    block = lax.broadcasted_iota(jnp.int32, (NB, LANES), 0)
    is_late = (block >= base) & (block < base + LATE)

    def rows_of(part, line):
        return jnp.where(
            is_late, line_rows(late_spec, part, line), line_rows(spec_ref, part, line)
        )

    half = kept_refs[0].shape[0]
    for n, kept_ref in enumerate(kept_refs):
        for i in range(half):
            group = firsts_ref[n] + (i // CORE_STEP) * 2 * CORE_STEP + i % CORE_STEP
            kept_ref[i] = gram(rows_of, (group + core * CORE_STEP) * PACK)
            sent_ref[n * half + i] = gram(rows_of, (group + (1 - core) * CORE_STEP) * PACK)


def late_kernel(
    base_ref, corner_ref, where_ref, core_ref, firsts_ref, starts_ref,
    halves, window_ref, spec_ref, early_power_ref, piece_ref, power_ref, late_spec, sent_ref, *refs,
):
    kept_refs, series = refs[:-1], refs[-1]
    rows, base = piece_ref.shape[0], base_ref[0]
    origin = corner_ref[0] - rows
    series[pl.ds(rows, WINDOW), :] = window_ref[...]
    series[pl.ds(pl.multiple_of(where_ref[0] * rows - origin, 8), rows), :] = piece_ref[...]
    power = early_power_ref[...]
    for pair in range(LATE // 2):
        numbers = [base + 2 * pair + i for i in range(2)]
        blocks = [series[pl.ds(starts_ref[b] - origin, NFFT), :] for b in numbers]
        power = power + transform(halves, blocks, numbers, late_spec)
    power_ref[...] = power
    packed_quarters(base, core_ref[0], firsts_ref, spec_ref, late_spec, sent_ref, kept_refs)


def rest_kernel(base_ref, core_ref, firsts_ref, spec_ref, late_spec, sent_ref, *kept_refs):
    packed_quarters(base_ref[0], core_ref[0], firsts_ref, spec_ref, late_spec, sent_ref, kept_refs)


def quarter_shapes(quarters):
    half = NF // PACK // 4 // 2
    return [jax.ShapeDtypeStruct((n * half, NB, LANES), F32) for n in (quarters, *[1] * quarters)]


def late(base, corner, where, core, firsts, starts, halves, window, spec, power, piece):
    quarters = firsts.shape[0]
    smem, vmem = pl.BlockSpec(memory_space=SMEM), pl.BlockSpec(memory_space=VMEM)
    return pl.pallas_call(
        late_kernel,
        name="late",
        in_specs=[smem] * 6 + [vmem] * 5,
        out_specs=[vmem] * (3 + quarters),
        out_shape=[jax.ShapeDtypeStruct(a.shape, F32) for a in (power, spec)]
        + quarter_shapes(quarters),
        scratch_shapes=[VMEM((2 * piece.shape[0] + WINDOW, LANES), F32)],
        compiler_params=pltpu.CompilerParams(vmem_limit_bytes=20 << 20),
        cost_estimate=pl.CostEstimate(flops=3 << 30, bytes_accessed=8 << 20, transcendentals=0),
    )(base, corner, where, core, firsts, starts, halves, window, spec, power, piece)


def rest(base, core, firsts, spec, late_spec):
    quarters = firsts.shape[0]
    smem, vmem = pl.BlockSpec(memory_space=SMEM), pl.BlockSpec(memory_space=VMEM)
    return pl.pallas_call(
        rest_kernel,
        name="rest",
        in_specs=[smem] * 3 + [vmem] * 2,
        out_specs=[vmem] * (1 + quarters),
        out_shape=quarter_shapes(quarters),
        compiler_params=pltpu.CompilerParams(vmem_limit_bytes=20 << 20),
        cost_estimate=pl.CostEstimate(flops=2 << 30, bytes_accessed=4 << 20, transcendentals=0),
    )(base, core, firsts, spec, late_spec)


def whole_kernel(starts_ref, table_ref, series_ref, power_ref, packed_ref, halves, spec):
    split_table(table_ref, halves)
    power_ref[...] = jnp.zeros_like(power_ref)

    def step(pair, carry):
        numbers = [2 * pair + i for i in range(2)]
        blocks = [series_ref[pl.ds(starts_ref[b], NFFT), :] for b in numbers]
        power_ref[...] += transform(halves, blocks, numbers, spec)
        return carry

    lax.fori_loop(0, NB // 2, step, 0, unroll=4)

    def step_gram(group, carry):
        packed_ref[group] = gram(functools.partial(line_rows, spec), group * PACK)
        return carry

    lax.fori_loop(0, NF // PACK, step_gram, 0, unroll=8)


def whole(starts, table, series):
    smem, vmem = pl.BlockSpec(memory_space=SMEM), pl.BlockSpec(memory_space=VMEM)
    return pl.pallas_call(
        whole_kernel,
        name="whole",
        in_specs=[smem, vmem, vmem],
        out_specs=[vmem] * 2,
        out_shape=[
            jax.ShapeDtypeStruct((NF, LANES), F32),
            jax.ShapeDtypeStruct((NF // PACK, NB, LANES), F32),
        ],
        scratch_shapes=[VMEM((2 * NFFT, NFFT), BF16), VMEM((2 * NF * PITCH, LANES), F32)],
        compiler_params=pltpu.CompilerParams(vmem_limit_bytes=28 << 20),
    )(starts, table, series)


def unpack_kernel(factor, order_ref, packed_ref, power_ref, *refs):
    out_ref, power_out, matrices, sems = refs[-4:]
    first = len(refs) == 4
    power_copy = pltpu.make_async_copy(power_ref, power_out, sems.at[1])
    if first:
        power_copy.start()
    row = lax.broadcasted_iota(jnp.int32, (NB, NB), 0)
    column = lax.broadcasted_iota(jnp.int32, (NB, NB), 1)
    count = packed_ref.shape[0]
    for j in range(count):
        packed = packed_ref[j] * factor
        turned = packed.T
        for i in range(PACK):
            here = packed[:, i * NB : (i + 1) * NB]
            there = turned[i * NB : (i + 1) * NB, :]
            matrices[0, j * PACK + i] = jnp.where(row <= column, here, there)
            matrices[1, j * PACK + i] = jnp.where(
                row > column, here, jnp.where(row < column, -there, 0.0)
            )
    lines = count * PACK
    copy = pltpu.make_async_copy(
        matrices, out_ref.at[:, pl.ds(order_ref[0] * lines, lines)], sems.at[0]
    )
    copy.start()
    copy.wait()
    if first:
        power_copy.wait()


def unpack(parts, order, power, factor):
    lines = parts[0].shape[0] * PACK
    anywhere = pl.BlockSpec(memory_space=pl.ANY)
    out = []
    for n, part in enumerate(parts):
        out = pl.pallas_call(
            functools.partial(unpack_kernel, factor),
            name="unpack",
            in_specs=[pl.BlockSpec(memory_space=SMEM), pl.BlockSpec(memory_space=VMEM)]
            + [pl.BlockSpec(memory_space=VMEM) if not out else anywhere]
            + [anywhere] * len(out[:1]),
            out_specs=[anywhere] * 2,
            out_shape=[
                jax.ShapeDtypeStruct((2, len(parts) * lines, NB, NB), F32),
                jax.ShapeDtypeStruct(power.shape, F32),
            ],
            input_output_aliases={3: 0, 2: 1} if out else {},
            scratch_shapes=[VMEM((2, lines, NB, NB), F32), pltpu.SemaphoreType.DMA((2,))],
            compiler_params=pltpu.CompilerParams(vmem_limit_bytes=8 << 20),
        )(order[n].reshape(1), part, out[1] if out else power, *out[:1])
    return out[1], out[0]


def swap(value, axis, bits):
    return lax.ppermute(value, axis, [(i, i ^ bits) for i in range(lax.axis_size(axis))])


def spread_small(snapshots, starts, table):
    me = lax.axis_index("tm")
    core = lax.axis_index("space") % 2
    z, x = me // 2, me % 2
    order = (4, 2, 1, 5, 3, 6, 7)
    rows = snapshots.shape[0]
    *pieces, own = cut((*order, 0), snapshots)
    pieces = [swap(p, "tm", k) for p, k in zip(pieces, order)]
    pieces, last = pieces[:-1] + [own], pieces[-1]
    where = jnp.stack([me ^ k for k in (*order[:-1], 0)])
    late_part = me ^ order[-1]
    before = jnp.sum((starts + (NFFT - 1) < late_part * rows).astype(jnp.int32))
    base = jnp.minimum(before, NB - LATE)
    corner = jnp.minimum(starts[base] // 8 * 8, lax.axis_size("tm") * rows - WINDOW).reshape(1)
    base = base.reshape(1)
    window, spec, power, halves = early(base, corner, where, starts, table, pieces)
    groups = NF // PACK // 4
    away = (3, 2, 1)
    firsts = jnp.stack([(z ^ j) * groups for j in (*away, 0)])
    core_number = core.reshape(1)
    power, late_spec, sent, *kept = late(
        base, corner, late_part.reshape(1), core_number, firsts[:2], starts,
        halves, window, spec, power, last,
    )
    sent_rest, *kept_rest = rest(base, core_number, firsts[2:], spec, late_spec)
    half = groups // 2
    terms = []
    for sent, kept in ((sent, kept), (sent_rest, kept_rest)):
        theirs = swap(sent, "space", 1)
        terms += [k + theirs[n * half : (n + 1) * half] for n, k in enumerate(kept)]
    terms = [swap(t, "tm", 2 * j) for j, t in zip(away, terms)] + terms[-1:]
    lower, upper = (sum(t[i * half // 2 : (i + 1) * half // 2] for t in terms) for i in range(2))
    mine, other = jnp.where(x == 0, lower, upper), jnp.where(x == 0, upper, lower)
    from_y = swap(mine, "space", 2)
    from_x = swap(other, "tm", 1)
    from_xy = lax.ppermute(
        other,
        ("tm", "space"),
        [(i * 4 + s, (i ^ 1) * 4 + (s ^ 2)) for i in range(8) for s in range(4)],
    )
    mine = mine + from_y + from_x + from_xy
    return power, [mine, swap(mine, "space", 1)], [core, 1 - core]


def spread_any(snapshots, starts, table):
    groups = lax.axis_size("tm")
    arranged = snapshots.reshape(snapshots.shape[0], groups, -1)
    series = lax.all_to_all(arranged, "tm", split_axis=1, concat_axis=0, tiled=True)[:, 0, :]
    power, packed = whole(starts, table, series)
    own = lax.psum_scatter(packed, "tm", scatter_dimension=0, tiled=True)
    return power, [lax.psum(own, "space")], [jnp.int32(0)]


def body(snapshots, starts, freq_lines):
    groups = lax.axis_size("tm")
    spaces = lax.axis_size("space")
    table = spectral_table(freq_lines)
    spread = spread_small if (groups, spaces) == (8, 4) else spread_any
    power, parts, order = spread(snapshots, starts, table)
    return unpack(parts, order, power, 1.0 / (NB * snapshots.shape[1] * spaces))


def solution(mesh):
    placed = (P("tm", "space"), P(), P())
    return jax.shard_map(
        body,
        mesh=mesh,
        in_specs=placed,
        out_specs=(P(None, ("space", "tm")), P(None, "tm", None, None)),
        check_vma=False,
    )
```

```python
import functools
import math

import jax
import jax.numpy as jnp
from jax import lax
from jax.experimental import pallas as pl
from jax.experimental.pallas import tpu as pltpu
from jax.sharding import PartitionSpec as P

NFFT = 256
NF = 128
NB = 32
LANES = 128
PACK = LANES // NB
PITCH = NB + 8
LATE = 8
WINDOW = (LATE - 1) * NFFT // 2 + NFFT // 2 + NFFT + 8
CORE_STEP = 2
F32 = jnp.float32
BF16 = jnp.bfloat16
VMEM = pltpu.VMEM
SMEM = pltpu.SMEM


def spectral_table(freq_lines):
    moments = jnp.arange(NFFT, dtype=jnp.int32)
    cycle = freq_lines[:, None] * moments[None, :] % NFFT
    angles = 2.0 * math.pi / NFFT * cycle.astype(jnp.float32)
    window = 0.5 - 0.5 * jnp.cos(2.0 * math.pi / NFFT * moments.astype(jnp.float32))
    window = window / jnp.sqrt(jnp.sum(window * window))
    return jnp.concatenate(
        [window[None, :] * jnp.cos(angles), -window[None, :] * jnp.sin(angles)], axis=0
    )


def split(x):
    high = x.astype(BF16)
    return high, (x - high.astype(F32)).astype(BF16)


def transform(halves, blocks, numbers, spec_ref):
    x_high, x_low = split(jnp.concatenate(blocks, axis=1))
    both = jnp.dot(halves[...], x_high, preferred_element_type=F32)
    out = jnp.dot(halves[:NFFT], x_low, preferred_element_type=F32)
    out = out + both[:NFFT] + both[NFFT:]
    power = []
    for i, b in enumerate(numbers):
        part = out[:, i * LANES : (i + 1) * LANES]
        spec_ref[pl.ds(b, 2 * NF, stride=PITCH), :] = part
        square = part * part
        power.append(square[:NF] + square[NF:])
    return (power[0] + power[1]) * (1.0 / NB)


def split_table(table_ref, halves):
    high, low = split(table_ref[...])
    halves[:NFFT] = high
    halves[NFFT:] = low


def gram(rows_of, line):
    rows = PACK * NB
    row = lax.broadcasted_iota(jnp.int32, (rows, LANES), 0) % NB
    lane = lax.broadcasted_iota(jnp.int32, (rows, LANES), 1)
    spectra = jnp.concatenate(
        [
            jnp.concatenate([rows_of(part, line + i) for i in range(PACK)], axis=0)
            for part in range(2)
        ],
        axis=1,
    )
    high, low = split(spectra)
    turned = jnp.concatenate([high[:, LANES:], -high[:, :LANES]], axis=1)
    both = lax.dot_general(
        jnp.concatenate([high, low], axis=0),
        jnp.concatenate([high, turned], axis=0),
        (((1,), (1,)), ((), ())),
        preferred_element_type=F32,
    )
    cross = both[rows:]
    mirrored = jnp.where(row >= lane % NB, cross[:, :LANES], -cross[:, LANES:])
    full = both[:rows] + cross
    full = jnp.where(row <= lane % NB, full[:, :LANES], full[:, LANES:]) + mirrored.T
    packed = full[:NB]
    for i in range(1, PACK):
        packed = jnp.where(lane[:NB] // NB == i, full[i * NB : (i + 1) * NB], packed)
    return packed


def line_rows(spec_ref, part, line):
    return spec_ref[pl.ds(pl.multiple_of((part * NF + line) * PITCH, 8), NB), :]


def cut_kernel(order, snapshots_ref, *refs):
    me = lax.axis_index("tm")
    pieces, sems = refs[:-1], refs[-1]
    copies = [
        pltpu.make_async_copy(
            snapshots_ref.at[:, pl.ds(pl.multiple_of((me ^ k) * LANES, LANES), LANES)],
            piece,
            sems.at[i],
        )
        for i, (k, piece) in enumerate(zip(order, pieces))
    ]
    for copy in copies:
        copy.start()
    for copy in copies:
        copy.wait()


def cut(order, snapshots):
    rows = snapshots.shape[0]
    grant = 52 if len(order) == 1 else 50
    return pl.pallas_call(
        functools.partial(cut_kernel, order),
        name="cut",
        in_specs=[pl.BlockSpec(memory_space=pltpu.HBM)],
        out_specs=[pl.BlockSpec(memory_space=VMEM)] * len(order),
        out_shape=[jax.ShapeDtypeStruct((rows, LANES), F32)] * len(order),
        scratch_shapes=[pltpu.SemaphoreType.DMA((len(order),))],
        compiler_params=pltpu.CompilerParams(vmem_limit_bytes=grant << 20),
        cost_estimate=pl.CostEstimate(
            flops=len(order) << 30, bytes_accessed=len(order) << 20, transcendentals=0
        ),
    )(snapshots)


def early_kernel(rows, base_ref, corner_ref, where_ref, starts_ref, table_ref, *refs):
    pieces, (window_ref, spec_ref, power_ref, halves, series) = refs[:-5], refs[-5:]
    for k, piece in enumerate(pieces):
        series[pl.ds(pl.multiple_of(where_ref[k] * rows, 8), rows), :] = piece[...]
    window_ref[...] = series[pl.ds(pl.multiple_of(corner_ref[0], 8), WINDOW), :]
    split_table(table_ref, halves)
    power_ref[...] = jnp.zeros_like(power_ref)

    def step(pair, carry):
        numbers = [2 * pair + i for i in range(2)]
        numbers = [jnp.where(b < base_ref[0], b, b + LATE) for b in numbers]
        blocks = [series[pl.ds(starts_ref[b], NFFT), :] for b in numbers]
        power_ref[...] += transform(halves, blocks, numbers, spec_ref)
        return carry

    lax.fori_loop(0, (NB - LATE) // 2, step, 0, unroll=4)


def early(base, corner, where, starts, table, pieces):
    rows = pieces[0].shape[0]
    smem, vmem = pl.BlockSpec(memory_space=SMEM), pl.BlockSpec(memory_space=VMEM)
    return pl.pallas_call(
        functools.partial(early_kernel, rows),
        name="early",
        in_specs=[smem] * 4 + [vmem] * (1 + len(pieces)),
        out_specs=[vmem] * 4,
        out_shape=[
            jax.ShapeDtypeStruct((WINDOW, LANES), F32),
            jax.ShapeDtypeStruct((2 * NF * PITCH, LANES), F32),
            jax.ShapeDtypeStruct((NF, LANES), F32),
            jax.ShapeDtypeStruct((2 * NFFT, NFFT), BF16),
        ],
        scratch_shapes=[VMEM(((len(pieces) + 1) * rows, LANES), F32)],
        compiler_params=pltpu.CompilerParams(vmem_limit_bytes=20 << 20),
        cost_estimate=pl.CostEstimate(
            flops=6 * 2 * NF * NFFT * (NB - LATE) * LANES, bytes_accessed=4 << 20, transcendentals=0
        ),
    )(base, corner, where, starts, table, *pieces)


def packed_quarters(base, core, firsts_ref, spec_ref, late_spec, sent_ref, kept_refs):
    block = lax.broadcasted_iota(jnp.int32, (NB, LANES), 0)
    is_late = (block >= base) & (block < base + LATE)

    def rows_of(part, line):
        return jnp.where(
            is_late, line_rows(late_spec, part, line), line_rows(spec_ref, part, line)
        )

    half = kept_refs[0].shape[0]
    for n, kept_ref in enumerate(kept_refs):
        for i in range(half):
            group = firsts_ref[n] + (i // CORE_STEP) * 2 * CORE_STEP + i % CORE_STEP
            kept_ref[i] = gram(rows_of, (group + core * CORE_STEP) * PACK)
            sent_ref[n * half + i] = gram(rows_of, (group + (1 - core) * CORE_STEP) * PACK)


def late_kernel(
    base_ref, corner_ref, where_ref, core_ref, firsts_ref, starts_ref,
    halves, window_ref, spec_ref, early_power_ref, piece_ref, power_ref, late_spec, sent_ref, *refs,
):
    kept_refs, series = refs[:-1], refs[-1]
    rows, base = piece_ref.shape[0], base_ref[0]
    origin = corner_ref[0] - rows
    series[pl.ds(rows, WINDOW), :] = window_ref[...]
    series[pl.ds(pl.multiple_of(where_ref[0] * rows - origin, 8), rows), :] = piece_ref[...]
    power = early_power_ref[...]
    for pair in range(LATE // 2):
        numbers = [base + 2 * pair + i for i in range(2)]
        blocks = [series[pl.ds(starts_ref[b] - origin, NFFT), :] for b in numbers]
        power = power + transform(halves, blocks, numbers, late_spec)
    power_ref[...] = power
    packed_quarters(base, core_ref[0], firsts_ref, spec_ref, late_spec, sent_ref, kept_refs)


def rest_kernel(base_ref, core_ref, firsts_ref, spec_ref, late_spec, sent_ref, *kept_refs):
    packed_quarters(base_ref[0], core_ref[0], firsts_ref, spec_ref, late_spec, sent_ref, kept_refs)


def quarter_shapes(quarters):
    half = NF // PACK // 4 // 2
    return [jax.ShapeDtypeStruct((n * half, NB, LANES), F32) for n in (quarters, *[1] * quarters)]


def late(base, corner, where, core, firsts, starts, halves, window, spec, power, piece):
    quarters = firsts.shape[0]
    smem, vmem = pl.BlockSpec(memory_space=SMEM), pl.BlockSpec(memory_space=VMEM)
    return pl.pallas_call(
        late_kernel,
        name="late",
        in_specs=[smem] * 6 + [vmem] * 5,
        out_specs=[vmem] * (3 + quarters),
        out_shape=[jax.ShapeDtypeStruct(a.shape, F32) for a in (power, spec)]
        + quarter_shapes(quarters),
        scratch_shapes=[VMEM((2 * piece.shape[0] + WINDOW, LANES), F32)],
        compiler_params=pltpu.CompilerParams(vmem_limit_bytes=20 << 20),
        cost_estimate=pl.CostEstimate(flops=3 << 30, bytes_accessed=8 << 20, transcendentals=0),
    )(base, corner, where, core, firsts, starts, halves, window, spec, power, piece)


def rest(base, core, firsts, spec, late_spec):
    quarters = firsts.shape[0]
    smem, vmem = pl.BlockSpec(memory_space=SMEM), pl.BlockSpec(memory_space=VMEM)
    return pl.pallas_call(
        rest_kernel,
        name="rest",
        in_specs=[smem] * 3 + [vmem] * 2,
        out_specs=[vmem] * (1 + quarters),
        out_shape=quarter_shapes(quarters),
        compiler_params=pltpu.CompilerParams(vmem_limit_bytes=20 << 20),
        cost_estimate=pl.CostEstimate(flops=2 << 30, bytes_accessed=4 << 20, transcendentals=0),
    )(base, core, firsts, spec, late_spec)


def whole_kernel(starts_ref, table_ref, series_ref, power_ref, packed_ref, halves, spec):
    split_table(table_ref, halves)
    power_ref[...] = jnp.zeros_like(power_ref)

    def step(pair, carry):
        numbers = [2 * pair + i for i in range(2)]
        blocks = [series_ref[pl.ds(starts_ref[b], NFFT), :] for b in numbers]
        power_ref[...] += transform(halves, blocks, numbers, spec)
        return carry

    lax.fori_loop(0, NB // 2, step, 0, unroll=4)

    def step_gram(group, carry):
        packed_ref[group] = gram(functools.partial(line_rows, spec), group * PACK)
        return carry

    lax.fori_loop(0, NF // PACK, step_gram, 0, unroll=8)


def whole(starts, table, series):
    smem, vmem = pl.BlockSpec(memory_space=SMEM), pl.BlockSpec(memory_space=VMEM)
    return pl.pallas_call(
        whole_kernel,
        name="whole",
        in_specs=[smem, vmem, vmem],
        out_specs=[vmem] * 2,
        out_shape=[
            jax.ShapeDtypeStruct((NF, LANES), F32),
            jax.ShapeDtypeStruct((NF // PACK, NB, LANES), F32),
        ],
        scratch_shapes=[VMEM((2 * NFFT, NFFT), BF16), VMEM((2 * NF * PITCH, LANES), F32)],
        compiler_params=pltpu.CompilerParams(vmem_limit_bytes=28 << 20),
    )(starts, table, series)


def unpack_kernel(factor, order_ref, packed_ref, power_ref, *refs):
    out_ref, power_out, matrices, sems = refs[-4:]
    first = len(refs) == 4
    power_copy = pltpu.make_async_copy(power_ref, power_out, sems.at[1])
    if first:
        power_copy.start()
    row = lax.broadcasted_iota(jnp.int32, (NB, NB), 0)
    column = lax.broadcasted_iota(jnp.int32, (NB, NB), 1)
    count = packed_ref.shape[0]
    for j in range(count):
        packed = packed_ref[j] * factor
        turned = packed.T
        for i in range(PACK):
            here = packed[:, i * NB : (i + 1) * NB]
            there = turned[i * NB : (i + 1) * NB, :]
            matrices[0, j * PACK + i] = jnp.where(row <= column, here, there)
            matrices[1, j * PACK + i] = jnp.where(
                row > column, here, jnp.where(row < column, -there, 0.0)
            )
    lines = count * PACK
    copy = pltpu.make_async_copy(
        matrices, out_ref.at[:, pl.ds(order_ref[0] * lines, lines)], sems.at[0]
    )
    copy.start()
    copy.wait()
    if first:
        power_copy.wait()


def unpack(parts, order, power, factor):
    lines = parts[0].shape[0] * PACK
    anywhere = pl.BlockSpec(memory_space=pl.ANY)
    out = []
    for n, part in enumerate(parts):
        out = pl.pallas_call(
            functools.partial(unpack_kernel, factor),
            name="unpack",
            in_specs=[pl.BlockSpec(memory_space=SMEM), pl.BlockSpec(memory_space=VMEM)]
            + [pl.BlockSpec(memory_space=VMEM) if not out else anywhere]
            + [anywhere] * len(out[:1]),
            out_specs=[anywhere] * 2,
            out_shape=[
                jax.ShapeDtypeStruct((2, len(parts) * lines, NB, NB), F32),
                jax.ShapeDtypeStruct(power.shape, F32),
            ],
            input_output_aliases={3: 0, 2: 1} if out else {},
            scratch_shapes=[VMEM((2, lines, NB, NB), F32), pltpu.SemaphoreType.DMA((2,))],
            compiler_params=pltpu.CompilerParams(vmem_limit_bytes=8 << 20),
        )(order[n].reshape(1), part, out[1] if out else power, *out[:1])
    return out[1], out[0]


def swap(value, axis, bits):
    return lax.ppermute(value, axis, [(i, i ^ bits) for i in range(lax.axis_size(axis))])


def spread_small(snapshots, starts, table):
    me = lax.axis_index("tm")
    core = lax.axis_index("space") % 2
    z, x = me // 2, me % 2
    order = (4, 2, 1, 5, 3, 6, 7)
    rows = snapshots.shape[0]
    (first,) = cut(order[:1], snapshots)
    first = swap(first, "tm", order[0])
    *pieces, own = cut((*order[1:], 0), snapshots)
    pieces = [first] + [swap(p, "tm", k) for p, k in zip(pieces, order[1:])]
    pieces, last = pieces[:-1] + [own], pieces[-1]
    where = jnp.stack([me ^ k for k in (*order[:-1], 0)])
    late_part = me ^ order[-1]
    before = jnp.sum((starts + (NFFT - 1) < late_part * rows).astype(jnp.int32))
    base = jnp.minimum(before, NB - LATE)
    corner = jnp.minimum(starts[base] // 8 * 8, lax.axis_size("tm") * rows - WINDOW).reshape(1)
    base = base.reshape(1)
    window, spec, power, halves = early(base, corner, where, starts, table, pieces)
    groups = NF // PACK // 4
    away = (3, 2, 1)
    firsts = jnp.stack([(z ^ j) * groups for j in (*away, 0)])
    core_number = core.reshape(1)
    power, late_spec, sent, *kept = late(
        base, corner, late_part.reshape(1), core_number, firsts[:2], starts,
        halves, window, spec, power, last,
    )
    sent_rest, *kept_rest = rest(base, core_number, firsts[2:], spec, late_spec)
    half = groups // 2
    terms = []
    for sent, kept in ((sent, kept), (sent_rest, kept_rest)):
        theirs = swap(sent, "space", 1)
        terms += [k + theirs[n * half : (n + 1) * half] for n, k in enumerate(kept)]
    terms = [swap(t, "tm", 2 * j) for j, t in zip(away, terms)] + terms[-1:]
    lower, upper = (sum(t[i * half // 2 : (i + 1) * half // 2] for t in terms) for i in range(2))
    mine, other = jnp.where(x == 0, lower, upper), jnp.where(x == 0, upper, lower)
    from_y = swap(mine, "space", 2)
    from_x = swap(other, "tm", 1)
    from_xy = lax.ppermute(
        other,
        ("tm", "space"),
        [(i * 4 + s, (i ^ 1) * 4 + (s ^ 2)) for i in range(8) for s in range(4)],
    )
    mine = mine + from_y + from_x + from_xy
    return power, [mine, swap(mine, "space", 1)], [core, 1 - core]


def spread_any(snapshots, starts, table):
    groups = lax.axis_size("tm")
    arranged = snapshots.reshape(snapshots.shape[0], groups, -1)
    series = lax.all_to_all(arranged, "tm", split_axis=1, concat_axis=0, tiled=True)[:, 0, :]
    power, packed = whole(starts, table, series)
    own = lax.psum_scatter(packed, "tm", scatter_dimension=0, tiled=True)
    return power, [lax.psum(own, "space")], [jnp.int32(0)]


def body(snapshots, starts, freq_lines):
    groups = lax.axis_size("tm")
    spaces = lax.axis_size("space")
    table = spectral_table(freq_lines)
    spread = spread_small if (groups, spaces) == (8, 4) else spread_any
    power, parts, order = spread(snapshots, starts, table)
    return unpack(parts, order, power, 1.0 / (NB * snapshots.shape[1] * spaces))


def solution(mesh):
    placed = (P("tm", "space"), P(), P())
    return jax.shard_map(
        body,
        mesh=mesh,
        in_specs=placed,
        out_specs=(P(None, ("space", "tm")), P(None, "tm", None, None)),
        check_vma=False,
    )
```

```python
import functools
import math

import jax
import jax.numpy as jnp
from jax import lax
from jax.experimental import pallas as pl
from jax.experimental.pallas import tpu as pltpu
from jax.sharding import PartitionSpec as P

NFFT = 256
NF = 128
NB = 32
LANES = 128
PACK = LANES // NB
PITCH = NB + 8
LATE = 8
WINDOW = (LATE - 1) * NFFT // 2 + NFFT // 2 + NFFT + 8
SPEC_ROWS = (2 * NF + 1) * PITCH
CORE_STEP = 2
F32 = jnp.float32
BF16 = jnp.bfloat16
VMEM = pltpu.VMEM
SMEM = pltpu.SMEM


def spectral_table(freq_lines):
    moments = jnp.arange(NFFT, dtype=jnp.int32)
    cycle = freq_lines[:, None] * moments[None, :] % NFFT
    angles = 2.0 * math.pi / NFFT * cycle.astype(jnp.float32)
    window = 0.5 - 0.5 * jnp.cos(2.0 * math.pi / NFFT * moments.astype(jnp.float32))
    window = window / jnp.sqrt(jnp.sum(window * window))
    return jnp.concatenate(
        [window[None, :] * jnp.cos(angles), -window[None, :] * jnp.sin(angles)], axis=0
    )


def split(x):
    high = x.astype(BF16)
    return high, (x - high.astype(F32)).astype(BF16)


def transform(halves, blocks, numbers, spec_ref):
    x_high, x_low = split(jnp.concatenate(blocks, axis=1))
    both = jnp.dot(halves[...], x_high, preferred_element_type=F32)
    out = jnp.dot(halves[:NFFT], x_low, preferred_element_type=F32)
    out = out + both[:NFFT] + both[NFFT:]
    power = []
    for i, b in enumerate(numbers):
        part = out[:, i * LANES : (i + 1) * LANES]
        spec_ref[pl.ds(b, 2 * NF, stride=PITCH), :] = part
        square = part * part
        power.append(square[:NF] + square[NF:])
    return (power[0] + power[1]) * (1.0 / NB)


def split_table(table_ref, halves):
    high, low = split(table_ref[...])
    halves[:NFFT] = high
    halves[NFFT:] = low


def gram(rows_of, line):
    rows = PACK * NB
    row = lax.broadcasted_iota(jnp.int32, (rows, LANES), 0) % NB
    lane = lax.broadcasted_iota(jnp.int32, (rows, LANES), 1)
    spectra = jnp.concatenate(
        [
            jnp.concatenate([rows_of(part, line + i) for i in range(PACK)], axis=0)
            for part in range(2)
        ],
        axis=1,
    )
    high, low = split(spectra)
    turned = jnp.concatenate([high[:, LANES:], -high[:, :LANES]], axis=1)
    both = lax.dot_general(
        jnp.concatenate([high, low], axis=0),
        jnp.concatenate([high, turned], axis=0),
        (((1,), (1,)), ((), ())),
        preferred_element_type=F32,
    )
    cross = both[rows:]
    mirrored = jnp.where(row >= lane % NB, cross[:, :LANES], -cross[:, LANES:])
    full = both[:rows] + cross
    full = jnp.where(row <= lane % NB, full[:, :LANES], full[:, LANES:]) + mirrored.T
    packed = full[:NB]
    for i in range(1, PACK):
        packed = jnp.where(lane[:NB] // NB == i, full[i * NB : (i + 1) * NB], packed)
    return packed


def line_rows(spec_ref, part, line):
    return spec_ref[pl.ds(pl.multiple_of((part * NF + line) * PITCH, 8), NB), :]


def cut_kernel(order, snapshots_ref, *refs):
    me = lax.axis_index("tm")
    pieces, sems = refs[:-1], refs[-1]
    copies = [
        pltpu.make_async_copy(
            snapshots_ref.at[:, pl.ds(pl.multiple_of((me ^ k) * LANES, LANES), LANES)],
            piece,
            sems.at[i],
        )
        for i, (k, piece) in enumerate(zip(order, pieces))
    ]
    for copy in copies:
        copy.start()
    for copy in copies:
        copy.wait()


def cut(order, snapshots):
    rows = snapshots.shape[0]
    grant = 52 if len(order) == 1 else 50
    return pl.pallas_call(
        functools.partial(cut_kernel, order),
        name="cut",
        in_specs=[pl.BlockSpec(memory_space=pltpu.HBM)],
        out_specs=[pl.BlockSpec(memory_space=VMEM)] * len(order),
        out_shape=[jax.ShapeDtypeStruct((rows, LANES), F32)] * len(order),
        scratch_shapes=[pltpu.SemaphoreType.DMA((len(order),))],
        compiler_params=pltpu.CompilerParams(vmem_limit_bytes=grant << 20),
        cost_estimate=pl.CostEstimate(
            flops=len(order) << 30, bytes_accessed=len(order) << 20, transcendentals=0
        ),
    )(snapshots)


def early_kernel(rows, base_ref, corner_ref, where_ref, starts_ref, table_ref, *refs):
    pieces, (window_ref, spec_ref, power_ref, halves, series) = refs[:-5], refs[-5:]
    for k, piece in enumerate(pieces):
        series[pl.ds(pl.multiple_of(where_ref[k] * rows, 8), rows), :] = piece[...]
    window_ref[...] = series[pl.ds(pl.multiple_of(corner_ref[0], 8), WINDOW), :]
    split_table(table_ref, halves)
    power_ref[...] = jnp.zeros_like(power_ref)

    def step(pair, carry):
        numbers = [2 * pair + i for i in range(2)]
        numbers = [jnp.where(b < base_ref[0], b, b + LATE) for b in numbers]
        blocks = [series[pl.ds(starts_ref[b], NFFT), :] for b in numbers]
        power_ref[...] += transform(halves, blocks, numbers, spec_ref)
        return carry

    lax.fori_loop(0, (NB - LATE) // 2, step, 0, unroll=4)


def early(base, corner, where, starts, table, pieces):
    rows = pieces[0].shape[0]
    smem, vmem = pl.BlockSpec(memory_space=SMEM), pl.BlockSpec(memory_space=VMEM)
    return pl.pallas_call(
        functools.partial(early_kernel, rows),
        name="early",
        in_specs=[smem] * 4 + [vmem] * (1 + len(pieces)),
        out_specs=[vmem] * 4,
        out_shape=[
            jax.ShapeDtypeStruct((WINDOW, LANES), F32),
            jax.ShapeDtypeStruct((SPEC_ROWS, LANES), F32),
            jax.ShapeDtypeStruct((NF, LANES), F32),
            jax.ShapeDtypeStruct((2 * NFFT, NFFT), BF16),
        ],
        scratch_shapes=[VMEM(((len(pieces) + 1) * rows, LANES), F32)],
        compiler_params=pltpu.CompilerParams(vmem_limit_bytes=20 << 20),
        cost_estimate=pl.CostEstimate(
            flops=6 * 2 * NF * NFFT * (NB - LATE) * LANES, bytes_accessed=4 << 20, transcendentals=0
        ),
    )(base, corner, where, starts, table, *pieces)


def packed_quarters(base, core, firsts_ref, spec_ref, late_spec, sent_ref, kept_refs):
    block = lax.broadcasted_iota(jnp.int32, (NB, LANES), 0)
    is_late = (block >= base) & (block < base + LATE)

    def rows_of(part, line):
        return jnp.where(
            is_late, line_rows(late_spec, part, line), line_rows(spec_ref, part, line)
        )

    half = kept_refs[0].shape[0]
    for n, kept_ref in enumerate(kept_refs):
        for i in range(half):
            group = firsts_ref[n] + (i // CORE_STEP) * 2 * CORE_STEP + i % CORE_STEP
            kept_ref[i] = gram(rows_of, (group + core * CORE_STEP) * PACK)
            sent_ref[n * half + i] = gram(rows_of, (group + (1 - core) * CORE_STEP) * PACK)


def late_kernel(
    base_ref, corner_ref, where_ref, core_ref, firsts_ref, starts_ref,
    halves, window_ref, spec_ref, early_power_ref, piece_ref, power_ref, late_spec, sent_ref, *refs,
):
    kept_refs, series = refs[:-1], refs[-1]
    rows, base = piece_ref.shape[0], base_ref[0]
    origin = corner_ref[0] - rows
    series[pl.ds(rows, WINDOW), :] = window_ref[...]
    series[pl.ds(pl.multiple_of(where_ref[0] * rows - origin, 8), rows), :] = piece_ref[...]
    power = early_power_ref[...]
    for pair in range(LATE // 2):
        numbers = [base + 2 * pair + i for i in range(2)]
        blocks = [series[pl.ds(starts_ref[b] - origin, NFFT), :] for b in numbers]
        power = power + transform(halves, blocks, numbers, late_spec)
    power_ref[...] = power
    packed_quarters(base, core_ref[0], firsts_ref, spec_ref, late_spec, sent_ref, kept_refs)


def rest_kernel(base_ref, core_ref, firsts_ref, spec_ref, late_spec, sent_ref, *kept_refs):
    packed_quarters(base_ref[0], core_ref[0], firsts_ref, spec_ref, late_spec, sent_ref, kept_refs)


def quarter_shapes(quarters):
    half = NF // PACK // 4 // 2
    return [jax.ShapeDtypeStruct((n * half, NB, LANES), F32) for n in (quarters, *[1] * quarters)]


def late(base, corner, where, core, firsts, starts, halves, window, spec, power, piece):
    quarters = firsts.shape[0]
    smem, vmem = pl.BlockSpec(memory_space=SMEM), pl.BlockSpec(memory_space=VMEM)
    return pl.pallas_call(
        late_kernel,
        name="late",
        in_specs=[smem] * 6 + [vmem] * 5,
        out_specs=[vmem] * (3 + quarters),
        out_shape=[jax.ShapeDtypeStruct(a.shape, F32) for a in (power, spec)]
        + quarter_shapes(quarters),
        scratch_shapes=[VMEM((2 * piece.shape[0] + WINDOW, LANES), F32)],
        compiler_params=pltpu.CompilerParams(vmem_limit_bytes=20 << 20),
        cost_estimate=pl.CostEstimate(flops=3 << 30, bytes_accessed=8 << 20, transcendentals=0),
    )(base, corner, where, core, firsts, starts, halves, window, spec, power, piece)


def rest(base, core, firsts, spec, late_spec):
    quarters = firsts.shape[0]
    smem, vmem = pl.BlockSpec(memory_space=SMEM), pl.BlockSpec(memory_space=VMEM)
    return pl.pallas_call(
        rest_kernel,
        name="rest",
        in_specs=[smem] * 3 + [vmem] * 2,
        out_specs=[vmem] * (1 + quarters),
        out_shape=quarter_shapes(quarters),
        compiler_params=pltpu.CompilerParams(vmem_limit_bytes=20 << 20),
        cost_estimate=pl.CostEstimate(flops=2 << 30, bytes_accessed=4 << 20, transcendentals=0),
    )(base, core, firsts, spec, late_spec)


def whole_kernel(starts_ref, table_ref, series_ref, power_ref, packed_ref, halves, spec):
    split_table(table_ref, halves)
    power_ref[...] = jnp.zeros_like(power_ref)

    def step(pair, carry):
        numbers = [2 * pair + i for i in range(2)]
        blocks = [series_ref[pl.ds(starts_ref[b], NFFT), :] for b in numbers]
        power_ref[...] += transform(halves, blocks, numbers, spec)
        return carry

    lax.fori_loop(0, NB // 2, step, 0, unroll=4)

    def step_gram(group, carry):
        packed_ref[group] = gram(functools.partial(line_rows, spec), group * PACK)
        return carry

    lax.fori_loop(0, NF // PACK, step_gram, 0, unroll=8)


def whole(starts, table, series):
    smem, vmem = pl.BlockSpec(memory_space=SMEM), pl.BlockSpec(memory_space=VMEM)
    return pl.pallas_call(
        whole_kernel,
        name="whole",
        in_specs=[smem, vmem, vmem],
        out_specs=[vmem] * 2,
        out_shape=[
            jax.ShapeDtypeStruct((NF, LANES), F32),
            jax.ShapeDtypeStruct((NF // PACK, NB, LANES), F32),
        ],
        scratch_shapes=[VMEM((2 * NFFT, NFFT), BF16), VMEM((SPEC_ROWS, LANES), F32)],
        compiler_params=pltpu.CompilerParams(vmem_limit_bytes=28 << 20),
    )(starts, table, series)


def unpack_kernel(factor, order_ref, packed_ref, power_ref, *refs):
    out_ref, power_out, matrices, sems = refs[-4:]
    first = len(refs) == 4
    if first:
        power_copy = pltpu.make_async_copy(power_ref, power_out, sems.at[1])
        power_copy.start()
    row = lax.broadcasted_iota(jnp.int32, (NB, NB), 0)
    column = lax.broadcasted_iota(jnp.int32, (NB, NB), 1)
    count = packed_ref.shape[0]
    for j in range(count):
        packed = packed_ref[j] * factor
        turned = packed.T
        for i in range(PACK):
            here = packed[:, i * NB : (i + 1) * NB]
            there = turned[i * NB : (i + 1) * NB, :]
            matrices[0, j * PACK + i] = jnp.where(row <= column, here, there)
            matrices[1, j * PACK + i] = jnp.where(
                row > column, here, jnp.where(row < column, -there, 0.0)
            )
    lines = count * PACK
    copy = pltpu.make_async_copy(
        matrices, out_ref.at[:, pl.ds(order_ref[0] * lines, lines)], sems.at[0]
    )
    copy.start()
    copy.wait()
    if first:
        power_copy.wait()


def unpack(parts, order, power, factor):
    lines = parts[0].shape[0] * PACK
    anywhere = pl.BlockSpec(memory_space=pl.ANY)
    out = []
    for n, part in enumerate(parts):
        out = pl.pallas_call(
            functools.partial(unpack_kernel, factor),
            name="unpack",
            in_specs=[pl.BlockSpec(memory_space=SMEM), pl.BlockSpec(memory_space=VMEM)]
            + [pl.BlockSpec(memory_space=VMEM) if not out else anywhere]
            + [anywhere] * len(out[:1]),
            out_specs=[anywhere] * 2,
            out_shape=[
                jax.ShapeDtypeStruct((2, len(parts) * lines, NB, NB), F32),
                jax.ShapeDtypeStruct(power.shape, F32),
            ],
            input_output_aliases={3: 0, 2: 1} if out else {},
            scratch_shapes=[VMEM((2, lines, NB, NB), F32), pltpu.SemaphoreType.DMA((2,))],
            compiler_params=pltpu.CompilerParams(vmem_limit_bytes=8 << 20),
        )(order[n].reshape(1), part, out[1] if out else power, *out[:1])
    return out[1], out[0]


def swap(value, axis, bits):
    return lax.ppermute(value, axis, [(i, i ^ bits) for i in range(lax.axis_size(axis))])


def spread_small(snapshots, starts, table):
    me = lax.axis_index("tm")
    core = lax.axis_index("space") % 2
    z, x = me // 2, me % 2
    order = (4, 2, 1, 5, 3, 6, 7)
    rows = snapshots.shape[0]
    (first,) = cut(order[:1], snapshots)
    first = swap(first, "tm", order[0])
    *pieces, own = cut((*order[1:], 0), snapshots)
    pieces = [first] + [swap(p, "tm", k) for p, k in zip(pieces, order[1:])]
    pieces, last = pieces[:-1] + [own], pieces[-1]
    where = jnp.stack([me ^ k for k in (*order[:-1], 0)])
    late_part = me ^ order[-1]
    before = jnp.sum((starts + (NFFT - 1) < late_part * rows).astype(jnp.int32))
    base = jnp.minimum(before, NB - LATE)
    corner = jnp.minimum(starts[base] // 8 * 8, lax.axis_size("tm") * rows - WINDOW).reshape(1)
    base = base.reshape(1)
    window, spec, power, halves = early(base, corner, where, starts, table, pieces)
    groups = NF // PACK // 4
    away = (3, 2, 1)
    firsts = jnp.stack([(z ^ j) * groups for j in (*away, 0)])
    core_number = core.reshape(1)
    power, late_spec, sent, *kept = late(
        base, corner, late_part.reshape(1), core_number, firsts[:2], starts,
        halves, window, spec, power, last,
    )
    sent_rest, *kept_rest = rest(base, core_number, firsts[2:], spec, late_spec)
    half = groups // 2
    terms = []
    for sent, kept in ((sent, kept), (sent_rest, kept_rest)):
        theirs = swap(sent, "space", 1)
        terms += [k + theirs[n * half : (n + 1) * half] for n, k in enumerate(kept)]
    terms = [swap(t, "tm", 2 * j) for j, t in zip(away, terms)] + terms[-1:]
    lower, upper = (sum(t[i * half // 2 : (i + 1) * half // 2] for t in terms) for i in range(2))
    mine, other = jnp.where(x == 0, lower, upper), jnp.where(x == 0, upper, lower)
    from_y = swap(mine, "space", 2)
    from_x = swap(other, "tm", 1)
    from_xy = lax.ppermute(
        other,
        ("tm", "space"),
        [(i * 4 + s, (i ^ 1) * 4 + (s ^ 2)) for i in range(8) for s in range(4)],
    )
    mine = mine + from_y + from_x + from_xy
    return power, [mine, swap(mine, "space", 1)], [core, 1 - core]


def spread_any(snapshots, starts, table):
    groups = lax.axis_size("tm")
    arranged = snapshots.reshape(snapshots.shape[0], groups, -1)
    series = lax.all_to_all(arranged, "tm", split_axis=1, concat_axis=0, tiled=True)[:, 0, :]
    power, packed = whole(starts, table, series)
    own = lax.psum_scatter(packed, "tm", scatter_dimension=0, tiled=True)
    return power, [lax.psum(own, "space")], [jnp.int32(0)]


def body(snapshots, starts, freq_lines):
    groups = lax.axis_size("tm")
    spaces = lax.axis_size("space")
    table = spectral_table(freq_lines)
    spread = spread_small if (groups, spaces) == (8, 4) else spread_any
    power, parts, order = spread(snapshots, starts, table)
    return unpack(parts, order, power, 1.0 / (NB * snapshots.shape[1] * spaces))


def solution(mesh):
    placed = (P("tm", "space"), P(), P())
    return jax.shard_map(
        body,
        mesh=mesh,
        in_specs=placed,
        out_specs=(P(None, ("space", "tm")), P(None, "tm", None, None)),
        check_vma=False,
    )
```

```python
import functools
import math

import jax
import jax.numpy as jnp
from jax import lax
from jax.experimental import pallas as pl
from jax.experimental.pallas import tpu as pltpu
from jax.sharding import PartitionSpec as P

NFFT = 256
NF = 128
NB = 32
LANES = 128
PACK = LANES // NB
PITCH = NB + 8
LATE = 8
WINDOW = (LATE - 1) * NFFT // 2 + NFFT // 2 + NFFT + 8
SPEC_ROWS = (2 * NF + 1) * PITCH
CORE_STEP = 2
F32 = jnp.float32
BF16 = jnp.bfloat16
VMEM = pltpu.VMEM
SMEM = pltpu.SMEM


def spectral_table(freq_lines):
    moments = jnp.arange(NFFT, dtype=jnp.int32)
    cycle = freq_lines[:, None] * moments[None, :] % NFFT
    angles = 2.0 * math.pi / NFFT * cycle.astype(jnp.float32)
    window = 0.5 - 0.5 * jnp.cos(2.0 * math.pi / NFFT * moments.astype(jnp.float32))
    window = window / jnp.sqrt(jnp.sum(window * window))
    return jnp.concatenate(
        [window[None, :] * jnp.cos(angles), -window[None, :] * jnp.sin(angles)], axis=0
    )


def split(x):
    high = x.astype(BF16)
    return high, (x - high.astype(F32)).astype(BF16)


def transform(halves, blocks, numbers, spec_ref):
    x_high, x_low = split(jnp.concatenate(blocks, axis=1))
    both = jnp.dot(halves[...], x_high, preferred_element_type=F32)
    out = jnp.dot(halves[:NFFT], x_low, preferred_element_type=F32)
    out = out + both[:NFFT] + both[NFFT:]
    power = []
    for i, b in enumerate(numbers):
        part = out[:, i * LANES : (i + 1) * LANES]
        spec_ref[pl.ds(b, 2 * NF, stride=PITCH), :] = part
        square = part * part
        power.append(square[:NF] + square[NF:])
    return (power[0] + power[1]) * (1.0 / NB)


def split_table(table_ref, halves):
    high, low = split(table_ref[...])
    halves[:NFFT] = high
    halves[NFFT:] = low


def gram(rows_of, line):
    rows = PACK * NB
    row = lax.broadcasted_iota(jnp.int32, (rows, LANES), 0) % NB
    lane = lax.broadcasted_iota(jnp.int32, (rows, LANES), 1)
    spectra = jnp.concatenate(
        [
            jnp.concatenate([rows_of(part, line + i) for i in range(PACK)], axis=0)
            for part in range(2)
        ],
        axis=1,
    )
    high, low = split(spectra)
    turned = jnp.concatenate([high[:, LANES:], -high[:, :LANES]], axis=1)
    both = lax.dot_general(
        jnp.concatenate([high, low], axis=0),
        jnp.concatenate([high, turned], axis=0),
        (((1,), (1,)), ((), ())),
        preferred_element_type=F32,
    )
    cross = both[rows:]
    mirrored = jnp.where(row >= lane % NB, cross[:, :LANES], -cross[:, LANES:])
    full = both[:rows] + cross
    full = jnp.where(row <= lane % NB, full[:, :LANES], full[:, LANES:]) + mirrored.T
    packed = full[:NB]
    for i in range(1, PACK):
        packed = jnp.where(lane[:NB] // NB == i, full[i * NB : (i + 1) * NB], packed)
    return packed


def line_rows(spec_ref, part, line):
    return spec_ref[pl.ds(pl.multiple_of((part * NF + line) * PITCH, 8), NB), :]


def cut_kernel(order, snapshots_ref, *refs):
    me = lax.axis_index("tm")
    pieces, sems = refs[:-1], refs[-1]
    copies = [
        pltpu.make_async_copy(
            snapshots_ref.at[:, pl.ds(pl.multiple_of((me ^ k) * LANES, LANES), LANES)],
            piece,
            sems.at[i],
        )
        for i, (k, piece) in enumerate(zip(order, pieces))
    ]
    for copy in copies:
        copy.start()
    for copy in copies:
        copy.wait()


def cut(order, snapshots):
    rows = snapshots.shape[0]
    grant = 52 if len(order) == 1 else 50
    return pl.pallas_call(
        functools.partial(cut_kernel, order),
        name="cut",
        in_specs=[pl.BlockSpec(memory_space=pltpu.HBM)],
        out_specs=[pl.BlockSpec(memory_space=VMEM)] * len(order),
        out_shape=[jax.ShapeDtypeStruct((rows, LANES), F32)] * len(order),
        scratch_shapes=[pltpu.SemaphoreType.DMA((len(order),))],
        compiler_params=pltpu.CompilerParams(vmem_limit_bytes=grant << 20),
        cost_estimate=pl.CostEstimate(
            flops=len(order) << 30, bytes_accessed=len(order) << 20, transcendentals=0
        ),
    )(snapshots)


def early_kernel(rows, base_ref, corner_ref, where_ref, starts_ref, table_ref, *refs):
    pieces, (window_ref, spec_ref, power_ref, halves, series) = refs[:-5], refs[-5:]
    for k, piece in enumerate(pieces):
        series[pl.ds(pl.multiple_of(where_ref[k] * rows, 8), rows), :] = piece[...]
    window_ref[...] = series[pl.ds(pl.multiple_of(corner_ref[0], 8), WINDOW), :]
    split_table(table_ref, halves)
    power_ref[...] = jnp.zeros_like(power_ref)

    def step(pair, carry):
        numbers = [2 * pair + i for i in range(2)]
        numbers = [jnp.where(b < base_ref[0], b, b + LATE) for b in numbers]
        blocks = [series[pl.ds(starts_ref[b], NFFT), :] for b in numbers]
        power_ref[...] += transform(halves, blocks, numbers, spec_ref)
        return carry

    lax.fori_loop(0, (NB - LATE) // 2, step, 0, unroll=4)


def early(base, corner, where, starts, table, pieces):
    rows = pieces[0].shape[0]
    smem, vmem = pl.BlockSpec(memory_space=SMEM), pl.BlockSpec(memory_space=VMEM)
    return pl.pallas_call(
        functools.partial(early_kernel, rows),
        name="early",
        in_specs=[smem] * 4 + [vmem] * (1 + len(pieces)),
        out_specs=[vmem] * 4,
        out_shape=[
            jax.ShapeDtypeStruct((WINDOW, LANES), F32),
            jax.ShapeDtypeStruct((SPEC_ROWS, LANES), F32),
            jax.ShapeDtypeStruct((NF, LANES), F32),
            jax.ShapeDtypeStruct((2 * NFFT, NFFT), BF16),
        ],
        scratch_shapes=[VMEM(((len(pieces) + 1) * rows, LANES), F32)],
        compiler_params=pltpu.CompilerParams(vmem_limit_bytes=20 << 20),
        cost_estimate=pl.CostEstimate(
            flops=6 * 2 * NF * NFFT * (NB - LATE) * LANES, bytes_accessed=4 << 20, transcendentals=0
        ),
    )(base, corner, where, starts, table, *pieces)


def packed_quarters(base, core, firsts_ref, spec_ref, late_spec, place):
    block = lax.broadcasted_iota(jnp.int32, (NB, LANES), 0)
    is_late = (block >= base) & (block < base + LATE)

    def rows_of(part, line):
        return jnp.where(
            is_late, line_rows(late_spec, part, line), line_rows(spec_ref, part, line)
        )

    quarters = firsts_ref.shape[0]
    for n in range(quarters):
        for i in range(NF // PACK // quarters // 2):
            group = firsts_ref[n] + (i // CORE_STEP) * 2 * CORE_STEP + i % CORE_STEP
            place(n, i, gram(rows_of, (group + core * CORE_STEP) * PACK))


def late_kernel(
    base_ref, corner_ref, where_ref, core_ref, firsts_ref, starts_ref,
    halves, window_ref, spec_ref, early_power_ref, piece_ref, power_ref, late_spec, sent_ref, series,
):
    rows, base = piece_ref.shape[0], base_ref[0]
    origin = corner_ref[0] - rows
    series[pl.ds(rows, WINDOW), :] = window_ref[...]
    series[pl.ds(pl.multiple_of(where_ref[0] * rows - origin, 8), rows), :] = piece_ref[...]
    power = early_power_ref[...]
    for pair in range(LATE // 2):
        numbers = [base + 2 * pair + i for i in range(2)]
        blocks = [series[pl.ds(starts_ref[b] - origin, NFFT), :] for b in numbers]
        power = power + transform(halves, blocks, numbers, late_spec)
    power_ref[...] = power
    half = sent_ref.shape[0] // firsts_ref.shape[0]

    def place(n, i, matrices):
        sent_ref[n * half + i] = matrices

    packed_quarters(base, 1 - core_ref[0], firsts_ref, spec_ref, late_spec, place)


def rest_kernel(base_ref, core_ref, firsts_ref, spec_ref, late_spec, *kept_refs):
    def place(n, i, matrices):
        kept_refs[n][i] = matrices

    packed_quarters(base_ref[0], core_ref[0], firsts_ref, spec_ref, late_spec, place)


def late(base, corner, where, core, firsts, starts, halves, window, spec, power, piece):
    smem, vmem = pl.BlockSpec(memory_space=SMEM), pl.BlockSpec(memory_space=VMEM)
    return pl.pallas_call(
        late_kernel,
        name="late",
        in_specs=[smem] * 6 + [vmem] * 5,
        out_specs=[vmem] * 3,
        out_shape=[jax.ShapeDtypeStruct(a.shape, F32) for a in (power, spec)]
        + [jax.ShapeDtypeStruct((NF // PACK // 2, NB, LANES), F32)],
        scratch_shapes=[VMEM((2 * piece.shape[0] + WINDOW, LANES), F32)],
        compiler_params=pltpu.CompilerParams(vmem_limit_bytes=20 << 20),
        cost_estimate=pl.CostEstimate(flops=3 << 30, bytes_accessed=8 << 20, transcendentals=0),
    )(base, corner, where, core, firsts, starts, halves, window, spec, power, piece)


def rest(base, core, firsts, spec, late_spec):
    quarters = firsts.shape[0]
    smem, vmem = pl.BlockSpec(memory_space=SMEM), pl.BlockSpec(memory_space=VMEM)
    return pl.pallas_call(
        rest_kernel,
        name="rest",
        in_specs=[smem] * 3 + [vmem] * 2,
        out_specs=[vmem] * quarters,
        out_shape=[jax.ShapeDtypeStruct((NF // PACK // quarters // 2, NB, LANES), F32)] * quarters,
        compiler_params=pltpu.CompilerParams(vmem_limit_bytes=20 << 20),
        cost_estimate=pl.CostEstimate(flops=2 << 30, bytes_accessed=4 << 20, transcendentals=0),
    )(base, core, firsts, spec, late_spec)


def whole_kernel(starts_ref, table_ref, series_ref, power_ref, packed_ref, halves, spec):
    split_table(table_ref, halves)
    power_ref[...] = jnp.zeros_like(power_ref)

    def step(pair, carry):
        numbers = [2 * pair + i for i in range(2)]
        blocks = [series_ref[pl.ds(starts_ref[b], NFFT), :] for b in numbers]
        power_ref[...] += transform(halves, blocks, numbers, spec)
        return carry

    lax.fori_loop(0, NB // 2, step, 0, unroll=4)

    def step_gram(group, carry):
        packed_ref[group] = gram(functools.partial(line_rows, spec), group * PACK)
        return carry

    lax.fori_loop(0, NF // PACK, step_gram, 0, unroll=8)


def whole(starts, table, series):
    smem, vmem = pl.BlockSpec(memory_space=SMEM), pl.BlockSpec(memory_space=VMEM)
    return pl.pallas_call(
        whole_kernel,
        name="whole",
        in_specs=[smem, vmem, vmem],
        out_specs=[vmem] * 2,
        out_shape=[
            jax.ShapeDtypeStruct((NF, LANES), F32),
            jax.ShapeDtypeStruct((NF // PACK, NB, LANES), F32),
        ],
        scratch_shapes=[VMEM((2 * NFFT, NFFT), BF16), VMEM((SPEC_ROWS, LANES), F32)],
        compiler_params=pltpu.CompilerParams(vmem_limit_bytes=28 << 20),
    )(starts, table, series)


def unpack_kernel(factor, order_ref, packed_ref, power_ref, *refs):
    out_ref, power_out, matrices, sems = refs[-4:]
    first = len(refs) == 4
    if first:
        power_copy = pltpu.make_async_copy(power_ref, power_out, sems.at[1])
        power_copy.start()
    row = lax.broadcasted_iota(jnp.int32, (NB, NB), 0)
    column = lax.broadcasted_iota(jnp.int32, (NB, NB), 1)
    count = packed_ref.shape[0]
    for j in range(count):
        packed = packed_ref[j] * factor
        turned = packed.T
        for i in range(PACK):
            here = packed[:, i * NB : (i + 1) * NB]
            there = turned[i * NB : (i + 1) * NB, :]
            matrices[0, j * PACK + i] = jnp.where(row <= column, here, there)
            matrices[1, j * PACK + i] = jnp.where(
                row > column, here, jnp.where(row < column, -there, 0.0)
            )
    lines = count * PACK
    copy = pltpu.make_async_copy(
        matrices, out_ref.at[:, pl.ds(order_ref[0] * lines, lines)], sems.at[0]
    )
    copy.start()
    copy.wait()
    if first:
        power_copy.wait()


def unpack(parts, order, power, factor):
    lines = parts[0].shape[0] * PACK
    anywhere = pl.BlockSpec(memory_space=pl.ANY)
    out = []
    for n, part in enumerate(parts):
        out = pl.pallas_call(
            functools.partial(unpack_kernel, factor),
            name="unpack",
            in_specs=[pl.BlockSpec(memory_space=SMEM), pl.BlockSpec(memory_space=VMEM)]
            + [pl.BlockSpec(memory_space=VMEM) if not out else anywhere]
            + [anywhere] * len(out[:1]),
            out_specs=[anywhere] * 2,
            out_shape=[
                jax.ShapeDtypeStruct((2, len(parts) * lines, NB, NB), F32),
                jax.ShapeDtypeStruct(power.shape, F32),
            ],
            input_output_aliases={3: 0, 2: 1} if out else {},
            scratch_shapes=[VMEM((2, lines, NB, NB), F32), pltpu.SemaphoreType.DMA((2,))],
            compiler_params=pltpu.CompilerParams(vmem_limit_bytes=8 << 20),
        )(order[n].reshape(1), part, out[1] if out else power, *out[:1])
    return out[1], out[0]


def swap(value, axis, bits):
    return lax.ppermute(value, axis, [(i, i ^ bits) for i in range(lax.axis_size(axis))])


def spread_small(snapshots, starts, table):
    me = lax.axis_index("tm")
    core = lax.axis_index("space") % 2
    z, x = me // 2, me % 2
    order = (4, 2, 1, 5, 3, 6, 7)
    rows = snapshots.shape[0]
    (first,) = cut(order[:1], snapshots)
    first = swap(first, "tm", order[0])
    *pieces, own = cut((*order[1:], 0), snapshots)
    pieces = [first] + [swap(p, "tm", k) for p, k in zip(pieces, order[1:])]
    pieces, last = pieces[:-1] + [own], pieces[-1]
    where = jnp.stack([me ^ k for k in (*order[:-1], 0)])
    late_part = me ^ order[-1]
    before = jnp.sum((starts + (NFFT - 1) < late_part * rows).astype(jnp.int32))
    base = jnp.minimum(before, NB - LATE)
    corner = jnp.minimum(starts[base] // 8 * 8, lax.axis_size("tm") * rows - WINDOW).reshape(1)
    base = base.reshape(1)
    window, spec, power, halves = early(base, corner, where, starts, table, pieces)
    groups = NF // PACK // 4
    away = (3, 2, 1)
    firsts = jnp.stack([(z ^ j) * groups for j in (*away, 0)])
    core_number = core.reshape(1)
    power, late_spec, sent = late(
        base, corner, late_part.reshape(1), core_number, firsts, starts,
        halves, window, spec, power, last,
    )
    kept = rest(base, core_number, firsts, spec, late_spec)
    half = groups // 2
    theirs = swap(sent, "space", 1)
    terms = [k + theirs[n * half : (n + 1) * half] for n, k in enumerate(kept)]
    terms = [swap(t, "tm", 2 * j) for j, t in zip(away, terms)] + terms[-1:]
    lower, upper = (sum(t[i * half // 2 : (i + 1) * half // 2] for t in terms) for i in range(2))
    mine, other = jnp.where(x == 0, lower, upper), jnp.where(x == 0, upper, lower)
    from_y = swap(mine, "space", 2)
    from_x = swap(other, "tm", 1)
    from_xy = lax.ppermute(
        other,
        ("tm", "space"),
        [(i * 4 + s, (i ^ 1) * 4 + (s ^ 2)) for i in range(8) for s in range(4)],
    )
    mine = mine + from_y + from_x + from_xy
    return power, [mine, swap(mine, "space", 1)], [core, 1 - core]


def spread_any(snapshots, starts, table):
    groups = lax.axis_size("tm")
    arranged = snapshots.reshape(snapshots.shape[0], groups, -1)
    series = lax.all_to_all(arranged, "tm", split_axis=1, concat_axis=0, tiled=True)[:, 0, :]
    power, packed = whole(starts, table, series)
    own = lax.psum_scatter(packed, "tm", scatter_dimension=0, tiled=True)
    return power, [lax.psum(own, "space")], [jnp.int32(0)]


def body(snapshots, starts, freq_lines):
    groups = lax.axis_size("tm")
    spaces = lax.axis_size("space")
    table = spectral_table(freq_lines)
    spread = spread_small if (groups, spaces) == (8, 4) else spread_any
    power, parts, order = spread(snapshots, starts, table)
    return unpack(parts, order, power, 1.0 / (NB * snapshots.shape[1] * spaces))


def solution(mesh):
    placed = (P("tm", "space"), P(), P())
    return jax.shard_map(
        body,
        mesh=mesh,
        in_specs=placed,
        out_specs=(P(None, ("space", "tm")), P(None, "tm", None, None)),
        check_vma=False,
    )
```

```python
import functools
import math

import jax
import jax.numpy as jnp
from jax import lax
from jax.experimental import pallas as pl
from jax.experimental.pallas import tpu as pltpu
from jax.sharding import PartitionSpec as P

NFFT = 256
NF = 128
NB = 32
LANES = 128
PACK = LANES // NB
PITCH = NB + 8
LATE = 8
WINDOW = (LATE - 1) * NFFT // 2 + NFFT // 2 + NFFT + 8
SPEC_ROWS = (2 * NF + 1) * PITCH
CORE_STEP = 2
F32 = jnp.float32
BF16 = jnp.bfloat16
VMEM = pltpu.VMEM
SMEM = pltpu.SMEM


def spectral_table(freq_lines):
    moments = jnp.arange(NFFT, dtype=jnp.int32)
    cycle = freq_lines[:, None] * moments[None, :] % NFFT
    angles = 2.0 * math.pi / NFFT * cycle.astype(jnp.float32)
    window = 0.5 - 0.5 * jnp.cos(2.0 * math.pi / NFFT * moments.astype(jnp.float32))
    window = window / jnp.sqrt(jnp.sum(window * window))
    return jnp.concatenate(
        [window[None, :] * jnp.cos(angles), -window[None, :] * jnp.sin(angles)], axis=0
    )


def split(x):
    high = x.astype(BF16)
    return high, (x - high.astype(F32)).astype(BF16)


def transform(halves, blocks, numbers, spec_ref):
    x_high, x_low = split(jnp.concatenate(blocks, axis=1))
    both = jnp.dot(halves[...], x_high, preferred_element_type=F32)
    out = jnp.dot(halves[:NFFT], x_low, preferred_element_type=F32)
    out = out + both[:NFFT] + both[NFFT:]
    power = []
    for i, b in enumerate(numbers):
        part = out[:, i * LANES : (i + 1) * LANES]
        spec_ref[pl.ds(b, 2 * NF, stride=PITCH), :] = part
        square = part * part
        power.append(square[:NF] + square[NF:])
    return (power[0] + power[1]) * (1.0 / NB)


def split_table(table_ref, halves):
    high, low = split(table_ref[...])
    halves[:NFFT] = high
    halves[NFFT:] = low


def gram(rows_of, line):
    rows = PACK * NB
    row = lax.broadcasted_iota(jnp.int32, (rows, LANES), 0) % NB
    lane = lax.broadcasted_iota(jnp.int32, (rows, LANES), 1)
    spectra = jnp.concatenate(
        [
            jnp.concatenate([rows_of(part, line + i) for i in range(PACK)], axis=0)
            for part in range(2)
        ],
        axis=1,
    )
    high, low = split(spectra)
    turned = jnp.concatenate([high[:, LANES:], -high[:, :LANES]], axis=1)
    both = lax.dot_general(
        jnp.concatenate([high, low], axis=0),
        jnp.concatenate([high, turned], axis=0),
        (((1,), (1,)), ((), ())),
        preferred_element_type=F32,
    )
    cross = both[rows:]
    mirrored = jnp.where(row >= lane % NB, cross[:, :LANES], -cross[:, LANES:])
    full = both[:rows] + cross
    full = jnp.where(row <= lane % NB, full[:, :LANES], full[:, LANES:]) + mirrored.T
    packed = full[:NB]
    for i in range(1, PACK):
        packed = jnp.where(lane[:NB] // NB == i, full[i * NB : (i + 1) * NB], packed)
    return packed


def line_rows(spec_ref, part, line):
    return spec_ref[pl.ds(pl.multiple_of((part * NF + line) * PITCH, 8), NB), :]


def cut_kernel(order, snapshots_ref, *refs):
    me = lax.axis_index("tm")
    pieces, sems = refs[:-1], refs[-1]
    copies = [
        pltpu.make_async_copy(
            snapshots_ref.at[:, pl.ds(pl.multiple_of((me ^ k) * LANES, LANES), LANES)],
            piece,
            sems.at[i],
        )
        for i, (k, piece) in enumerate(zip(order, pieces))
    ]
    for copy in copies:
        copy.start()
    for copy in copies:
        copy.wait()


def cut(order, snapshots):
    rows = snapshots.shape[0]
    grant = 52 if len(order) == 1 else 50
    return pl.pallas_call(
        functools.partial(cut_kernel, order),
        name="cut",
        in_specs=[pl.BlockSpec(memory_space=pltpu.HBM)],
        out_specs=[pl.BlockSpec(memory_space=VMEM)] * len(order),
        out_shape=[jax.ShapeDtypeStruct((rows, LANES), F32)] * len(order),
        scratch_shapes=[pltpu.SemaphoreType.DMA((len(order),))],
        compiler_params=pltpu.CompilerParams(vmem_limit_bytes=grant << 20),
        cost_estimate=pl.CostEstimate(
            flops=len(order) << 30, bytes_accessed=len(order) << 20, transcendentals=0
        ),
    )(snapshots)


def early_kernel(rows, base_ref, corner_ref, where_ref, starts_ref, table_ref, *refs):
    pieces, (window_ref, spec_ref, power_ref, halves, series) = refs[:-5], refs[-5:]
    for k, piece in enumerate(pieces):
        series[pl.ds(pl.multiple_of(where_ref[k] * rows, 8), rows), :] = piece[...]
    window_ref[...] = series[pl.ds(pl.multiple_of(corner_ref[0], 8), WINDOW), :]
    split_table(table_ref, halves)
    power_ref[...] = jnp.zeros_like(power_ref)

    def step(pair, carry):
        numbers = [2 * pair + i for i in range(2)]
        numbers = [jnp.where(b < base_ref[0], b, b + LATE) for b in numbers]
        blocks = [series[pl.ds(starts_ref[b], NFFT), :] for b in numbers]
        power_ref[...] += transform(halves, blocks, numbers, spec_ref)
        return carry

    lax.fori_loop(0, (NB - LATE) // 2, step, 0, unroll=4)


def early(base, corner, where, starts, table, pieces):
    rows = pieces[0].shape[0]
    smem, vmem = pl.BlockSpec(memory_space=SMEM), pl.BlockSpec(memory_space=VMEM)
    return pl.pallas_call(
        functools.partial(early_kernel, rows),
        name="early",
        in_specs=[smem] * 4 + [vmem] * (1 + len(pieces)),
        out_specs=[vmem] * 4,
        out_shape=[
            jax.ShapeDtypeStruct((WINDOW, LANES), F32),
            jax.ShapeDtypeStruct((SPEC_ROWS, LANES), F32),
            jax.ShapeDtypeStruct((NF, LANES), F32),
            jax.ShapeDtypeStruct((2 * NFFT, NFFT), BF16),
        ],
        scratch_shapes=[VMEM(((len(pieces) + 1) * rows, LANES), F32)],
        compiler_params=pltpu.CompilerParams(vmem_limit_bytes=20 << 20),
        cost_estimate=pl.CostEstimate(
            flops=6 * 2 * NF * NFFT * (NB - LATE) * LANES, bytes_accessed=4 << 20, transcendentals=0
        ),
    )(base, corner, where, starts, table, *pieces)


def packed_quarters(base, core, firsts_ref, spec_ref, late_spec, place):
    block = lax.broadcasted_iota(jnp.int32, (NB, LANES), 0)
    is_late = (block >= base) & (block < base + LATE)

    def rows_of(part, line):
        return jnp.where(
            is_late, line_rows(late_spec, part, line), line_rows(spec_ref, part, line)
        )

    quarters = firsts_ref.shape[0]
    for n in range(quarters):
        for i in range(NF // PACK // quarters // 2):
            group = firsts_ref[n] + (i // CORE_STEP) * 2 * CORE_STEP + i % CORE_STEP
            place(n, i, gram(rows_of, (group + core * CORE_STEP) * PACK))


def late_kernel(
    base_ref, corner_ref, where_ref, core_ref, firsts_ref, starts_ref,
    halves, window_ref, spec_ref, early_power_ref, piece_ref, power_ref, late_spec, sent_ref, series,
):
    rows, base = piece_ref.shape[0], base_ref[0]
    origin = corner_ref[0] - rows
    series[pl.ds(rows, WINDOW), :] = window_ref[...]
    series[pl.ds(pl.multiple_of(where_ref[0] * rows - origin, 8), rows), :] = piece_ref[...]
    power = early_power_ref[...]
    for pair in range(LATE // 2):
        numbers = [base + 2 * pair + i for i in range(2)]
        blocks = [series[pl.ds(starts_ref[b] - origin, NFFT), :] for b in numbers]
        power = power + transform(halves, blocks, numbers, late_spec)
    power_ref[...] = power
    half = sent_ref.shape[0] // firsts_ref.shape[0]

    def place(n, i, matrices):
        sent_ref[n * half + i] = matrices

    packed_quarters(base, 1 - core_ref[0], firsts_ref, spec_ref, late_spec, place)


def rest_kernel(base_ref, core_ref, firsts_ref, spec_ref, late_spec, *kept_refs):
    def place(n, i, matrices):
        kept_refs[n][i] = matrices

    packed_quarters(base_ref[0], core_ref[0], firsts_ref, spec_ref, late_spec, place)


def late(base, corner, where, core, firsts, starts, halves, window, spec, power, piece):
    smem, vmem = pl.BlockSpec(memory_space=SMEM), pl.BlockSpec(memory_space=VMEM)
    return pl.pallas_call(
        late_kernel,
        name="late",
        in_specs=[smem] * 6 + [vmem] * 5,
        out_specs=[vmem] * 3,
        out_shape=[jax.ShapeDtypeStruct(a.shape, F32) for a in (power, spec)]
        + [jax.ShapeDtypeStruct((NF // PACK // 2, NB, LANES), F32)],
        scratch_shapes=[VMEM((2 * piece.shape[0] + WINDOW, LANES), F32)],
        compiler_params=pltpu.CompilerParams(vmem_limit_bytes=20 << 20),
        cost_estimate=pl.CostEstimate(flops=3 << 30, bytes_accessed=8 << 20, transcendentals=0),
    )(base, corner, where, core, firsts, starts, halves, window, spec, power, piece)


def rest(base, core, firsts, spec, late_spec):
    quarters = firsts.shape[0]
    smem, vmem = pl.BlockSpec(memory_space=SMEM), pl.BlockSpec(memory_space=VMEM)
    return pl.pallas_call(
        rest_kernel,
        name="rest",
        in_specs=[smem] * 3 + [vmem] * 2,
        out_specs=[vmem] * quarters,
        out_shape=[jax.ShapeDtypeStruct((NF // PACK // quarters // 2, NB, LANES), F32)] * quarters,
        compiler_params=pltpu.CompilerParams(vmem_limit_bytes=20 << 20),
        cost_estimate=pl.CostEstimate(flops=2 << 30, bytes_accessed=4 << 20, transcendentals=0),
    )(base, core, firsts, spec, late_spec)


def whole_kernel(starts_ref, table_ref, series_ref, power_ref, packed_ref, halves, spec):
    split_table(table_ref, halves)
    power_ref[...] = jnp.zeros_like(power_ref)

    def step(pair, carry):
        numbers = [2 * pair + i for i in range(2)]
        blocks = [series_ref[pl.ds(starts_ref[b], NFFT), :] for b in numbers]
        power_ref[...] += transform(halves, blocks, numbers, spec)
        return carry

    lax.fori_loop(0, NB // 2, step, 0, unroll=4)

    def step_gram(group, carry):
        packed_ref[group] = gram(functools.partial(line_rows, spec), group * PACK)
        return carry

    lax.fori_loop(0, NF // PACK, step_gram, 0, unroll=8)


def whole(starts, table, series):
    smem, vmem = pl.BlockSpec(memory_space=SMEM), pl.BlockSpec(memory_space=VMEM)
    return pl.pallas_call(
        whole_kernel,
        name="whole",
        in_specs=[smem, vmem, vmem],
        out_specs=[vmem] * 2,
        out_shape=[
            jax.ShapeDtypeStruct((NF, LANES), F32),
            jax.ShapeDtypeStruct((NF // PACK, NB, LANES), F32),
        ],
        scratch_shapes=[VMEM((2 * NFFT, NFFT), BF16), VMEM((SPEC_ROWS, LANES), F32)],
        compiler_params=pltpu.CompilerParams(vmem_limit_bytes=28 << 20),
    )(starts, table, series)


def unpack_kernel(factor, order_ref, packed_ref, power_ref, *refs):
    out_ref, power_out, matrices, sems = refs[-4:]
    first = len(refs) == 4
    if first:
        power_copy = pltpu.make_async_copy(power_ref, power_out, sems.at[1])
        power_copy.start()
    row = lax.broadcasted_iota(jnp.int32, (NB, NB), 0)
    column = lax.broadcasted_iota(jnp.int32, (NB, NB), 1)
    count = packed_ref.shape[0]
    for j in range(count):
        packed = packed_ref[j] * factor
        turned = packed.T
        for i in range(PACK):
            here = packed[:, i * NB : (i + 1) * NB]
            there = turned[i * NB : (i + 1) * NB, :]
            matrices[0, j * PACK + i] = jnp.where(row <= column, here, there)
            matrices[1, j * PACK + i] = jnp.where(
                row > column, here, jnp.where(row < column, -there, 0.0)
            )
    lines = count * PACK
    copy = pltpu.make_async_copy(
        matrices, out_ref.at[:, pl.ds(order_ref[0] * lines, lines)], sems.at[0]
    )
    copy.start()
    copy.wait()
    if first:
        power_copy.wait()


def unpack(parts, order, power, factor):
    lines = parts[0].shape[0] * PACK
    anywhere = pl.BlockSpec(memory_space=pl.ANY)
    out = []
    for n, part in enumerate(parts):
        out = pl.pallas_call(
            functools.partial(unpack_kernel, factor),
            name="unpack",
            in_specs=[pl.BlockSpec(memory_space=SMEM), pl.BlockSpec(memory_space=VMEM)]
            + [pl.BlockSpec(memory_space=VMEM) if not out else anywhere]
            + [anywhere] * len(out[:1]),
            out_specs=[anywhere] * 2,
            out_shape=[
                jax.ShapeDtypeStruct((2, len(parts) * lines, NB, NB), F32),
                jax.ShapeDtypeStruct(power.shape, F32),
            ],
            input_output_aliases={3: 0, 2: 1} if out else {},
            scratch_shapes=[VMEM((2, lines, NB, NB), F32), pltpu.SemaphoreType.DMA((2,))],
            compiler_params=pltpu.CompilerParams(vmem_limit_bytes=8 << 20),
        )(order[n].reshape(1), part, out[1] if out else power, *out[:1])
    return out[1], out[0]


def swap(value, axis, bits):
    return lax.ppermute(value, axis, [(i, i ^ bits) for i in range(lax.axis_size(axis))])


def spread_small(snapshots, starts, table):
    me = lax.axis_index("tm")
    core = lax.axis_index("space") % 2
    z, x = me // 2, me % 2
    order = (4, 2, 1, 5, 3, 6, 7)
    rows = snapshots.shape[0]
    (first,) = cut(order[:1], snapshots)
    first = swap(first, "tm", order[0])
    *pieces, own = cut((*order[1:], 0), snapshots)
    pieces = [first] + [swap(p, "tm", k) for p, k in zip(pieces, order[1:])]
    pieces, last = pieces[:-1] + [own], pieces[-1]
    where = jnp.stack([me ^ k for k in (*order[:-1], 0)])
    late_part = me ^ order[-1]
    before = jnp.sum((starts + (NFFT - 1) < late_part * rows).astype(jnp.int32))
    base = jnp.minimum(before, NB - LATE)
    corner = jnp.minimum(starts[base] // 8 * 8, lax.axis_size("tm") * rows - WINDOW).reshape(1)
    base = base.reshape(1)
    window, spec, power, halves = early(base, corner, where, starts, table, pieces)
    groups = NF // PACK // 4
    away = (3, 1, 2)
    firsts = jnp.stack([(z ^ j) * groups for j in (*away, 0)])
    core_number = core.reshape(1)
    power, late_spec, sent = late(
        base, corner, late_part.reshape(1), core_number, firsts, starts,
        halves, window, spec, power, last,
    )
    kept = rest(base, core_number, firsts, spec, late_spec)
    half = groups // 2
    theirs = swap(sent, "space", 1)
    terms = [k + theirs[n * half : (n + 1) * half] for n, k in enumerate(kept)]
    terms = [swap(t, "tm", 2 * j) for j, t in zip(away, terms)] + terms[-1:]
    lower, upper = (sum(t[i * half // 2 : (i + 1) * half // 2] for t in terms) for i in range(2))
    mine, other = jnp.where(x == 0, lower, upper), jnp.where(x == 0, upper, lower)
    from_y = swap(mine, "space", 2)
    from_x = swap(other, "tm", 1)
    from_xy = lax.ppermute(
        other,
        ("tm", "space"),
        [(i * 4 + s, (i ^ 1) * 4 + (s ^ 2)) for i in range(8) for s in range(4)],
    )
    mine = mine + from_y + from_x + from_xy
    return power, [mine, swap(mine, "space", 1)], [core, 1 - core]


def spread_any(snapshots, starts, table):
    groups = lax.axis_size("tm")
    arranged = snapshots.reshape(snapshots.shape[0], groups, -1)
    series = lax.all_to_all(arranged, "tm", split_axis=1, concat_axis=0, tiled=True)[:, 0, :]
    power, packed = whole(starts, table, series)
    own = lax.psum_scatter(packed, "tm", scatter_dimension=0, tiled=True)
    return power, [lax.psum(own, "space")], [jnp.int32(0)]


def body(snapshots, starts, freq_lines):
    groups = lax.axis_size("tm")
    spaces = lax.axis_size("space")
    table = spectral_table(freq_lines)
    spread = spread_small if (groups, spaces) == (8, 4) else spread_any
    power, parts, order = spread(snapshots, starts, table)
    return unpack(parts, order, power, 1.0 / (NB * snapshots.shape[1] * spaces))


def solution(mesh):
    placed = (P("tm", "space"), P(), P())
    return jax.shard_map(
        body,
        mesh=mesh,
        in_specs=placed,
        out_specs=(P(None, ("space", "tm")), P(None, "tm", None, None)),
        check_vma=False,
    )
```
